32 devices in a mesh: expert: 8 (over z, x), shard: 4 (over y, core).
Axes of the slice: x: 2, y: 2, z: 4, core: 2. Of those that a mesh axis runs over, the one named last changes fastest.
Arguments:
- frames: bfloat16 [2048, 1024], P('expert', 'shard'), may hold values from -6 to 6
- expert_ids: int32 [2048, 2], P('expert'), may hold values from 0 to 7, all different within a row; in each aligned block of 256 rows (0 to 255, 256 to 511, ...) at most 96 rows name the same one
- gate_weights: float32 [2048, 2], P('expert'), may hold values from 0.2 to 1
- cotangent: bfloat16 [2048, 1024], P('expert', 'shard'), may hold values from -6 to 6
- weight_gate: bfloat16 [8, 1024, 6144], P('expert', None, 'shard'), may hold values from -0.1875 to 0.1875
- weight_up: bfloat16 [8, 1024, 6144], P('expert', None, 'shard'), may hold values from -0.1875 to 0.1875
- weight_down: bfloat16 [8, 6144, 1024], P('expert', 'shard'), may hold values from -0.078125 to 0.078125
Outputs:
- combined: bfloat16 [2048, 1024], P('expert', 'shard')
- frame_grad: bfloat16 [2048, 1024], P('expert', 'shard')
- grad_gate: bfloat16 [8, 1024, 6144], P('expert', None, 'shard')
- grad_up: bfloat16 [8, 1024, 6144], P('expert', None, 'shard')
- grad_down: bfloat16 [8, 6144, 1024], P('expert', 'shard')
The draws below stay inside these ranges and needn't reach their ends.
Inputs may be any that keep to these rules, and one draw needn't show every extreme that they name: `expert_ids`: each row names 2 different experts. In each aligned block of 256 rows (the frames of one index of expert) no expert is named by more than 96 rows, a bound that some block reaches.
All inputs are finite; a program needn't handle non-finite values.
Results may differ from the reference program's by a relative error of at most 0.018.
Values may be sent and summed in bfloat16 or wider, within the bound.
No kernel may reach another device: no remote copies, remote signals or barrier semaphores. Data moves between devices by JAX's collectives and lax.ppermute only.
A program may use at most 128 MiB of HBM per device.

```python
import math
import jax
import jax.numpy as jnp
import numpy as np
from jax import lax

D = 1024
FF = 6144
TOPK = 2
TOK = 256
EXPERTS = 8
CAP = 96
TOKENS = 2048
N_EXPERT = 8
N_SHARD = 4


def steps_of(stream_key, extent, split, smallest, largest):
    def one(axis_at, shards_of):
        steps = jax.random.uniform(jax.random.fold_in(jax.random.fold_in(stream_key, 6), axis_at), (shards_of,), jnp.float32, smallest / len(split), largest / len(split))
        return jnp.repeat(jnp.exp(steps), extent[axis_at] // shards_of).reshape((-1,) + (1,) * (len(extent) - axis_at - 1))

    loudness = one(*split[0])
    for cut in split[1:]:
        loudness = loudness * one(*cut)
    return loudness


def assign_block(rng, own, number, rows, count, top, reach, skew):
    ranking = jax.random.permutation(rng, count)
    crowded, ordinary = load_shares(count, rows * top, reach, skew, True), load_shares(count, rows * top, reach, skew, False)
    places = jnp.arange(count)

    def named(sizes, turn):
        used = int((sizes > 0).sum())
        fixed = max(1, used // 4)
        moved = fixed + (places - fixed + turn * (used - fixed)) % max(1, count - fixed)
        return jnp.zeros((count,), jnp.int32).at[ranking[jnp.where(places < fixed, places, moved)]].set(jnp.asarray(sizes, jnp.int32))

    sizes = jnp.where(number % 4 == 0, named(crowded, number // 4), named(ordinary, number - number // 4 - 1))
    mixed = jax.random.permutation(jax.random.fold_in(own, 3), count)
    donor, sink = mixed[0:count // 2 * 2:2], mixed[1:count // 2 * 2:2]
    room = jnp.minimum(sizes[donor] - 1, reach - sizes[sink]) // 2
    room = jnp.where((donor == ranking[0]) | (sink == ranking[0]) | (sizes[sink] == 0), 0, jnp.maximum(room, 0))
    moved = jax.random.randint(jax.random.fold_in(own, 4), (count // 2,), 0, 1 << 20) % (room + 1)
    sizes = sizes.at[donor].add(-moved).at[sink].add(moved)
    members = jnp.searchsorted(jnp.cumsum(sizes), jnp.arange(rows * top), side="right").astype(jnp.int32)
    listing = members.reshape(top, rows).T
    listing = listing[jax.random.permutation(jax.random.fold_in(own, 1), rows)]
    turn = jax.random.randint(jax.random.fold_in(own, 2), (rows, 1), 0, top)
    return jnp.take_along_axis(listing, (jnp.arange(top)[None, :] + turn) % top, axis=1)


def load_shares(number_of, total, limit, lean, full):
    portions = [(1 << 20) // math.isqrt(rank ** lean) + 1 for rank in range(1, number_of + 1)]
    largest = limit if full else min(limit, max(-(-total // number_of), total * portions[0] // sum(portions)))
    least = 1 if total - largest >= number_of - 1 else 0
    given, surplus = [largest] + [least] * (number_of - 1), total - largest - least * (number_of - 1)
    while surplus > 0:
        candidates = [i for i in range(1, number_of) if given[i] < largest] or [i for i in range(1, number_of) if given[i] < limit]
        whole, remaining = sum([portions[i] for i in candidates]), surplus
        for i in candidates:
            extra = min(limit - given[i], max(1, remaining * portions[i] // whole), surplus)
            given[i] = given[i] + extra
            surplus = surplus - extra
    return np.array(given)


def scatter_about(own_key, shape, scale, bound, split=(), kind=jnp.bfloat16):
    values = scale * jax.random.normal(own_key, shape, jnp.float32)
    if split:
        values = values * steps_of(own_key, shape, split, -0.22, 0.18)
    return jnp.clip(values, -bound, bound).astype(kind)


def setup_inputs(seed: int = 0) -> dict:
    streams_of = jax.random.split(jax.random.key(seed), 8)
    frames = scatter_about(streams_of[0], (TOKENS, D), 1.0, 6.0, ((0, 8), (1, 4)))
    expert_ids_keys = jax.random.split(jax.random.fold_in(streams_of[1], 1), TOKENS // TOK)
    expert_ids_turns = jax.random.permutation(jax.random.fold_in(streams_of[1], 3), TOKENS // TOK)
    expert_ids = jax.vmap(lambda own, number: assign_block(jax.random.fold_in(streams_of[1], 2), own, number, TOK, EXPERTS, TOPK, CAP, 2))(expert_ids_keys, expert_ids_turns).reshape((TOKENS, TOPK))
    gate_weights = jnp.clip(0.2 + 0.8 * jax.random.uniform(streams_of[2], (TOKENS, TOPK), jnp.float32) ** steps_of(streams_of[2], (TOKENS, TOPK), ((0, 8),), -0.2, 0.2), 0.2, 1.0)
    cotangent = scatter_about(streams_of[3], (TOKENS, D), 1.0, 6.0, ((0, 8), (1, 4)))
    weight_gate = scatter_about(streams_of[4], (EXPERTS, D, FF), D ** -0.5, 0.1875, ((0, 8), (2, 4)))
    weight_up = scatter_about(streams_of[5], (EXPERTS, D, FF), D ** -0.5, 0.1875, ((0, 8), (2, 4)))
    weight_down = scatter_about(streams_of[6], (EXPERTS, FF, D), FF ** -0.5, 0.078125, ((0, 8), (1, 4)))
    return dict(frames=frames, expert_ids=expert_ids, gate_weights=gate_weights, cotangent=cotangent, weight_gate=weight_gate, weight_up=weight_up, weight_down=weight_down)


def route_slot(expert_ids):
    grouped = expert_ids.reshape(N_EXPERT, TOK * TOPK)
    table = (grouped[:, :, None] == jnp.arange(EXPERTS, dtype=jnp.int32)[None, None, :]).astype(jnp.int32)
    earlier = jnp.cumsum(table, axis=1) - table
    return jnp.sum(earlier * table, axis=2).reshape(-1).astype(jnp.int32)


def rounded(values):
    return lax.optimization_barrier(values.astype(jnp.bfloat16)).astype(jnp.float32)


def expert_pass(operands):
    inputs, routed, gate_matrix, up_matrix, down_matrix = operands
    rows_count = inputs.shape[0]
    share = FF // N_SHARD
    input_wide = inputs.astype(jnp.float32)
    routed_wide = routed.astype(jnp.float32)
    gate_wide = gate_matrix.astype(jnp.float32)
    up_wide = up_matrix.astype(jnp.float32)
    down_wide = down_matrix.astype(jnp.float32)
    gate_act = jnp.dot(input_wide, gate_wide, preferred_element_type=jnp.float32)
    up_act = jnp.dot(input_wide, up_wide, preferred_element_type=jnp.float32)
    sigma_gate = jax.nn.sigmoid(gate_act)
    hidden = (gate_act * sigma_gate * up_act).astype(jnp.bfloat16)
    hidden_wide = hidden.astype(jnp.float32)
    out_terms = jnp.einsum("rsf,sfd->srd", hidden_wide.reshape(rows_count, N_SHARD, share), down_wide.reshape(N_SHARD, share, D))
    expert_out = jnp.sum(rounded(out_terms), axis=0)
    hidden_grad = jnp.dot(routed_wide, down_wide.T, preferred_element_type=jnp.float32)
    grad_down = jnp.dot(hidden_wide.T, routed_wide, preferred_element_type=jnp.float32).astype(jnp.bfloat16)
    gate_grad = (hidden_grad * up_act * sigma_gate * (1.0 + gate_act * (1.0 - sigma_gate))).astype(jnp.bfloat16)
    up_grad = (hidden_grad * gate_act * sigma_gate).astype(jnp.bfloat16)
    gate_grad_wide = gate_grad.astype(jnp.float32)
    up_grad_wide = up_grad.astype(jnp.float32)
    grad_gate = jnp.dot(input_wide.T, gate_grad_wide, preferred_element_type=jnp.float32).astype(jnp.bfloat16)
    grad_up = jnp.dot(input_wide.T, up_grad_wide, preferred_element_type=jnp.float32).astype(jnp.bfloat16)
    back_terms = jnp.einsum("rsf,dsf->srd", gate_grad_wide.reshape(rows_count, N_SHARD, share), gate_wide.reshape(D, N_SHARD, share))
    back_terms = back_terms + jnp.einsum("rsf,dsf->srd", up_grad_wide.reshape(rows_count, N_SHARD, share), up_wide.reshape(D, N_SHARD, share))
    expert_back = jnp.sum(rounded(back_terms), axis=0)
    return expert_out, expert_back, grad_gate, grad_up, grad_down


def reference(frames, expert_ids, gate_weights, cotangent, weight_gate, weight_up, weight_down):
    flat_ids = expert_ids.reshape(-1).astype(jnp.int32)
    slot_index = route_slot(expert_ids)
    anchor = (jnp.arange(TOKENS * TOPK, dtype=jnp.int32) // (TOK * TOPK)).astype(jnp.int32)
    row_index = (anchor * CAP + slot_index).astype(jnp.int32)
    weights_flat = gate_weights.reshape(-1, 1).astype(jnp.float32)
    frame_copies = jnp.repeat(frames, TOPK, axis=0)
    routed_cot = (jnp.repeat(cotangent, TOPK, axis=0).astype(jnp.float32) * weights_flat).astype(jnp.bfloat16)
    slots_total = N_EXPERT * CAP
    dispatched = jnp.zeros((EXPERTS, slots_total, D), jnp.bfloat16).at[flat_ids, row_index].set(frame_copies)
    routed_all = jnp.zeros((EXPERTS, slots_total, D), jnp.bfloat16).at[flat_ids, row_index].set(routed_cot)
    expert_out, expert_back, grad_gate, grad_up, grad_down = lax.map(expert_pass, (dispatched, routed_all, weight_gate, weight_up, weight_down))
    picked_out = expert_out[flat_ids, row_index]
    picked_back = expert_back[flat_ids, row_index]
    combined = jnp.sum((picked_out * weights_flat).reshape(TOKENS, TOPK, D), axis=1).astype(jnp.bfloat16)
    frame_grad = jnp.sum(picked_back.reshape(TOKENS, TOPK, D), axis=1).astype(jnp.bfloat16)
    return combined, frame_grad, grad_gate, grad_up, grad_down
```

```python
import functools

import jax
import jax.numpy as jnp
from jax import lax
from jax.experimental import pallas as pl
from jax.experimental.pallas import tpu as pltpu
from jax.sharding import PartitionSpec as P


F32, BF16, I32 = jnp.float32, jnp.bfloat16, jnp.int32
VMEM_LIMIT = 56 * 1024 * 1024


def contract(left, right, left_dim, right_dim):
    return lax.dot_general(
        left, right, (((left_dim,), (right_dim,)), ((), ())), preferred_element_type=F32
    )


def whole_block():
    return pl.BlockSpec(memory_space=pltpu.VMEM)


def scalar_block():
    return pl.BlockSpec(memory_space=pltpu.SMEM)


def selection(me, ids, experts, capacity):
    tok = ids.shape[1]
    expert_of = jnp.bitwise_xor(lax.broadcasted_iota(I32, (experts, tok), 0), me)
    first = ids[0:1, :] == expert_of
    second = ids[1:2, :] == expert_of
    table = jnp.where(first | second, 1.0, 0.0)
    upper = jnp.where(
        lax.broadcasted_iota(I32, (tok, tok), 0) < lax.broadcasted_iota(I32, (tok, tok), 1),
        1.0,
        0.0,
    )
    earlier = contract(table.astype(BF16), upper.astype(BF16), 1, 0).astype(I32)
    slot_first = jnp.where(first, earlier, -1)
    slot_second = jnp.where(second, earlier, -1)

    def one_hot(slots, k):
        rows = lax.broadcasted_iota(I32, (capacity, tok), 0)
        return jnp.where(slots[k : k + 1, :] == rows, 1.0, 0.0).astype(BF16)

    return slot_first, slot_second, one_hot


def dispatch_kernel(me_ref, ids_ref, gates_ref, frames_ref, cot_ref, *send_refs):
    experts = len(send_refs)
    capacity = send_refs[0].shape[0]
    width = frames_ref.shape[1]
    slot_first, slot_second, one_hot = selection(me_ref[0], ids_ref[...], experts, capacity)
    gates = jnp.transpose(jnp.concatenate([gates_ref[...]] * 4, axis=0))
    cot = cot_ref[...].astype(F32)
    weighted = jnp.concatenate(
        [(cot * gates[:, 0:1]).astype(BF16), (cot * gates[:, 1:2]).astype(BF16)], axis=0
    )
    frames = frames_ref[...]
    for k in range(experts):
        first, second = one_hot(slot_first, k), one_hot(slot_second, k)
        send_refs[k][:, :width] = contract(first + second, frames, 1, 0).astype(BF16)
        send_refs[k][:, width:] = contract(
            jnp.concatenate([first, second], axis=1), weighted, 1, 0
        ).astype(BF16)


def dispatch(me, ids, gates, frames, cot, experts, capacity):
    width = 2 * frames.shape[1]
    return pl.pallas_call(
        dispatch_kernel,
        out_shape=[jax.ShapeDtypeStruct((capacity, width), BF16)] * experts,
        in_specs=[scalar_block()] + [whole_block()] * 4,
        out_specs=[whole_block()] * experts,
        compiler_params=pltpu.CompilerParams(vmem_limit_bytes=VMEM_LIMIT),
        name="dispatch",
    )(me, ids, gates, frames, cot)


def combine_kernel(me_ref, ids_ref, gates_ref, *refs):
    got_refs, (combined_ref, grad_ref) = refs[:-2], refs[-2:]
    experts = len(got_refs)
    capacity = got_refs[0].shape[0]
    width = combined_ref.shape[1]
    slot_first, slot_second, one_hot = selection(me_ref[0], ids_ref[...], experts, capacity)
    gates = jnp.transpose(jnp.concatenate([gates_ref[...]] * 4, axis=0))
    got = jnp.concatenate([ref[...] for ref in got_refs], axis=0)
    first = jnp.concatenate([one_hot(slot_first, k) for k in range(experts)], axis=0)
    second = jnp.concatenate([one_hot(slot_second, k) for k in range(experts)], axis=0)
    picked = contract(first, got, 0, 0), contract(second, got, 0, 0)
    combined_ref[...] = (
        picked[0][:, :width] * gates[:, 0:1] + picked[1][:, :width] * gates[:, 1:2]
    ).astype(BF16)
    grad_ref[...] = (picked[0][:, width:] + picked[1][:, width:]).astype(BF16)


def combine(me, ids, gates, got):
    tok, width = ids.shape[1], got[0].shape[1] // 2
    return pl.pallas_call(
        combine_kernel,
        out_shape=[jax.ShapeDtypeStruct((tok, width), BF16)] * 2,
        in_specs=[scalar_block()] + [whole_block()] * (2 + len(got)),
        out_specs=[whole_block()] * 2,
        compiler_params=pltpu.CompilerParams(vmem_limit_bytes=VMEM_LIMIT),
        name="combine",
    )(me, ids, gates, *got)


def pieces_of(ref, me, count, axis):
    size = ref.shape[axis] // count
    parts = []
    for j in range(count):
        start = pl.multiple_of(jnp.bitwise_xor(me, j) * size, size)
        parts.append(ref[pl.ds(start, size), :] if axis == 0 else ref[:, pl.ds(start, size)])
    return jnp.concatenate(parts, axis=axis)


def split_sums(me, count, sums_ref, keep_ref, send_ref):
    size = sums_ref.shape[1] // count
    for j in range(count):
        start = pl.multiple_of(jnp.bitwise_xor(me, j) * size, size)
        ref = send_ref if j % 2 else keep_ref
        ref[:, (j // 2) * size : (j // 2 + 1) * size] = sums_ref[:, pl.ds(start, size)].astype(BF16)


def forward_kernel(
    count, me_ref, *refs
):
    x_refs = refs[:count]
    gate_ref, up_ref, down_ref = refs[count : count + 3]
    hidden_ref, slope_ref, silu_ref, keep_ref, send_ref, sums_ref = refs[count + 3 :]
    step = pl.program_id(0)
    me = me_ref[0]
    inputs = jnp.concatenate([ref[...] for ref in x_refs], axis=1)
    gate_act = contract(inputs, pieces_of(gate_ref, me, count, 0), 1, 0)
    up_act = contract(inputs, pieces_of(up_ref, me, count, 0), 1, 0)
    sigma = jax.nn.sigmoid(gate_act)
    silu = gate_act * sigma
    hidden = (silu * up_act).astype(BF16)
    hidden_ref[...] = hidden
    silu_ref[...] = silu.astype(BF16)
    slope_ref[...] = (up_act * sigma * (1.0 + gate_act * (1.0 - sigma))).astype(BF16)
    product = contract(hidden, down_ref[...], 1, 0)

    @pl.when(step == 0)
    def _():
        sums_ref[...] = product

    @pl.when(step > 0)
    def _():
        sums_ref[...] += product

    @pl.when(step == pl.num_programs(0) - 1)
    def _():
        split_sums(me, count, sums_ref, keep_ref, send_ref)


def forward(me, x_parts, gate, up, down, tile):
    rows, part = x_parts[0].shape[0], x_parts[0].shape[1] // 2
    count, (model, hidden) = len(x_parts), gate.shape
    half = model // 2
    columns = pl.BlockSpec((model, tile), lambda i: (0, i))
    acts = pl.BlockSpec((rows, tile), lambda i: (0, i))
    fixed = lambda shape: pl.BlockSpec(shape, lambda i: (0, 0))
    return pl.pallas_call(
        functools.partial(forward_kernel, count),
        grid=(hidden // tile,),
        out_shape=[jax.ShapeDtypeStruct((rows, hidden), BF16)] * 3
        + [jax.ShapeDtypeStruct((rows, half), BF16)] * 2,
        in_specs=[scalar_block()]
        + [fixed((rows, part))] * count
        + [columns, columns, pl.BlockSpec((tile, model), lambda i: (i, 0))],
        out_specs=[acts] * 3 + [fixed((rows, half))] * 2,
        scratch_shapes=[pltpu.VMEM((rows, model), F32)],
        compiler_params=pltpu.CompilerParams(vmem_limit_bytes=VMEM_LIMIT),
        cost_estimate=pl.CostEstimate(
            flops=6 * rows * model * hidden, bytes_accessed=16 << 20, transcendentals=0
        ),
        name="forward",
    )(me, *x_parts, gate, up, down)


def backward_kernel(count, me_ref, *refs):
    c_refs = refs[:count]
    slope_ref, silu_ref, gate_ref, up_ref, down_ref = refs[count : count + 5]
    gate_grad_ref, up_grad_ref, keep_ref, send_ref, sums_ref = refs[count + 5 :]
    step = pl.program_id(0)
    me = me_ref[0]
    routed = jnp.concatenate([ref[...] for ref in c_refs], axis=1)
    hidden_grad = contract(routed, pieces_of(down_ref, me, count, 1), 1, 1)
    gate_grad = (hidden_grad * slope_ref[...].astype(F32)).astype(BF16)
    up_grad = (hidden_grad * silu_ref[...].astype(F32)).astype(BF16)
    gate_grad_ref[...] = gate_grad
    up_grad_ref[...] = up_grad
    product = contract(gate_grad, gate_ref[...], 1, 1) + contract(up_grad, up_ref[...], 1, 1)

    @pl.when(step == 0)
    def _():
        sums_ref[...] = product

    @pl.when(step > 0)
    def _():
        sums_ref[...] += product

    @pl.when(step == pl.num_programs(0) - 1)
    def _():
        split_sums(me, count, sums_ref, keep_ref, send_ref)


def backward(me, c_parts, slope, silu, gate, up, down, tile):
    rows, part = c_parts[0].shape[0], c_parts[0].shape[1] // 2
    count, (model, hidden) = len(c_parts), gate.shape
    half = model // 2
    columns = pl.BlockSpec((model, tile), lambda i: (0, i))
    acts = pl.BlockSpec((rows, tile), lambda i: (0, i))
    fixed = lambda shape: pl.BlockSpec(shape, lambda i: (0, 0))
    return pl.pallas_call(
        functools.partial(backward_kernel, count),
        grid=(hidden // tile,),
        out_shape=[jax.ShapeDtypeStruct((rows, hidden), BF16)] * 2
        + [jax.ShapeDtypeStruct((rows, half), BF16)] * 2,
        in_specs=[scalar_block()]
        + [pl.BlockSpec((rows, part), lambda i: (0, 1))] * count
        + [acts, acts, columns, columns, pl.BlockSpec((tile, model), lambda i: (i, 0))],
        out_specs=[acts] * 2 + [fixed((rows, half))] * 2,
        scratch_shapes=[pltpu.VMEM((rows, model), F32)],
        compiler_params=pltpu.CompilerParams(vmem_limit_bytes=VMEM_LIMIT),
        cost_estimate=pl.CostEstimate(
            flops=6 * rows * model * hidden, bytes_accessed=16 << 20, transcendentals=0
        ),
        name="backward",
    )(me, *c_parts, slope, silu, gate, up, down)


def weight_kernel(count, me_ref, *refs):
    xc_refs = refs[:count]
    hidden_ref, gate_grad_ref, up_grad_ref = refs[count : count + 3]
    grad_gate_ref, grad_up_ref, grad_down_ref, x_turned_ref = refs[count + 3 :]
    me = me_ref[0]
    part = xc_refs[0].shape[1] // 2

    @pl.when(pl.program_id(0) == 0)
    def _():
        for j in range(count):
            start = pl.multiple_of(jnp.bitwise_xor(me, j) * part, part)
            x_turned_ref[pl.ds(start, part), :] = jnp.transpose(xc_refs[j][:, :part])

    turned = x_turned_ref[...]
    grad_gate_ref[...] = contract(turned, gate_grad_ref[...], 1, 0).astype(BF16)
    grad_up_ref[...] = contract(turned, up_grad_ref[...], 1, 0).astype(BF16)
    hidden_turned = jnp.transpose(hidden_ref[...])
    for j in range(count):
        start = pl.multiple_of(jnp.bitwise_xor(me, j) * part, part)
        grad_down_ref[:, pl.ds(start, part)] = contract(
            hidden_turned, xc_refs[j][:, part:], 1, 0
        ).astype(BF16)


def weights(me, parts, hidden, gate_grad, up_grad, tile):
    rows, part = parts[0].shape[0], parts[0].shape[1] // 2
    count = len(parts)
    model, inner = count * part, hidden.shape[1]
    acts = pl.BlockSpec((rows, tile), lambda i: (0, i))
    columns = pl.BlockSpec((model, tile), lambda i: (0, i))
    return pl.pallas_call(
        functools.partial(weight_kernel, count),
        grid=(inner // tile,),
        out_shape=[jax.ShapeDtypeStruct((model, inner), BF16)] * 2
        + [jax.ShapeDtypeStruct((inner, model), BF16)],
        in_specs=[scalar_block()]
        + [pl.BlockSpec((rows, 2 * part), lambda i: (0, 0))] * count
        + [acts] * 3,
        out_specs=[columns, columns, pl.BlockSpec((tile, model), lambda i: (i, 0))],
        scratch_shapes=[pltpu.VMEM((model, rows), BF16)],
        compiler_params=pltpu.CompilerParams(vmem_limit_bytes=VMEM_LIMIT),
        cost_estimate=pl.CostEstimate(
            flops=6 * rows * model * inner, bytes_accessed=20 << 20, transcendentals=0
        ),
        name="weights",
    )(me, *parts, hidden, gate_grad, up_grad)


def swap(value, axis, bit):
    pairs = [(i, i ^ bit) for i in range(lax.axis_size(axis))]
    return lax.ppermute(value, axis, pairs)


def fast_device(frames, expert_ids, gate_weights, cotangent, weight_gate, weight_up, weight_down):
    experts, shards = lax.axis_size("expert"), lax.axis_size("shard")
    tok_rows, part = frames.shape
    capacity = 3 * tok_rows // experts
    expert_at = lax.axis_index("expert").astype(I32).reshape(1)
    shard_at = lax.axis_index("shard").astype(I32).reshape(1)
    ids, gates = expert_ids.T, gate_weights.T
    gate, up, down = weight_gate[0], weight_up[0], weight_down[0]
    tile = 256

    sent = dispatch(expert_at, ids, gates, frames, cotangent, experts, capacity)
    order = sorted(range(1, experts), reverse=True)
    got = {0: sent[0]}
    for k in order:
        got[k] = swap(sent[k], "expert", k)
    own = jnp.concatenate([got[k] for k in range(experts)], axis=0)

    parts = [own]
    bit = shards // 2
    while bit:
        parts = parts + [swap(p, "shard", bit) for p in parts]
        bit //= 2
    offsets = [0]
    bit = shards // 2
    while bit:
        offsets = offsets + [o ^ bit for o in offsets]
        bit //= 2
    parts = [parts[offsets.index(j)] for j in range(shards)]

    hidden, slope, silu, out_keep, out_send = forward(shard_at, parts, gate, up, down, tile)
    gate_grad, up_grad, back_keep, back_send = backward(
        shard_at, parts, slope, silu, gate, up, down, tile
    )
    grad_gate, grad_up, grad_down = weights(shard_at, parts, hidden, gate_grad, up_grad, tile)

    def scattered(keep, send):
        total = keep.astype(F32) + swap(send, "shard", 1).astype(F32)
        width = total.shape[1]
        bit = 2
        while bit < shards:
            width //= 2
            total = total[:, :width] + swap(
                total[:, width:].astype(BF16), "shard", bit
            ).astype(F32)
            bit *= 2
        return total.astype(BF16)

    out_rows = scattered(out_keep, out_send)
    back_rows = scattered(back_keep, back_send)
    both = jnp.concatenate([out_rows, back_rows], axis=1)
    returned = []
    for k in range(experts):
        piece = both[k * capacity : (k + 1) * capacity]
        returned.append(swap(piece, "expert", k) if k else piece)
    combined, frame_grad = combine(expert_at, ids, gates, returned)
    return combined, frame_grad, grad_gate[None], grad_up[None], grad_down[None]


def route_slot(flat_ids, experts):
    table = (flat_ids[:, None] == jnp.arange(experts, dtype=jnp.int32)[None, :]).astype(jnp.int32)
    earlier = jnp.cumsum(table, axis=0) - table
    return jnp.sum(earlier * table, axis=1)


def plain_device(frames, expert_ids, gate_weights, cotangent, weight_gate, weight_up, weight_down):
    experts = lax.axis_size("expert")
    tok_rows = frames.shape[0]
    top_count = expert_ids.shape[1]
    capacity = 3 * tok_rows // experts
    total_rows = experts * capacity
    part = frames.shape[1]
    flat_ids = expert_ids.reshape(-1)
    targets = flat_ids * capacity + route_slot(flat_ids, experts)
    weights_flat = gate_weights.reshape(-1, 1)
    gate, up, down = weight_gate[0], weight_up[0], weight_down[0]

    def exchange(values):
        return lax.all_to_all(values, "expert", split_axis=0, concat_axis=0, tiled=True)

    def place_rows(values):
        return jnp.zeros((total_rows, part), values.dtype).at[targets].set(values)

    frame_rows = jnp.repeat(frames, top_count, axis=0)
    cot_rows = jnp.repeat(cotangent, top_count, axis=0).astype(F32) * weights_flat
    inputs, routed = (
        lax.all_gather(exchange(place_rows(rows)), "shard", axis=1, tiled=True)
        for rows in (frame_rows, cot_rows.astype(BF16))
    )
    gate_act, up_act = contract(inputs, gate, 1, 0), contract(inputs, up, 1, 0)
    sigma = jax.nn.sigmoid(gate_act)
    hidden = (gate_act * sigma * up_act).astype(BF16)
    out_part = contract(hidden, down, 1, 0)
    hidden_grad = contract(routed, down, 1, 1)
    grad_down = contract(hidden, routed, 0, 0).astype(BF16)
    gate_grad = (hidden_grad * up_act * sigma * (1.0 + gate_act * (1.0 - sigma))).astype(BF16)
    up_grad = (hidden_grad * gate_act * sigma).astype(BF16)
    grad_gate = contract(inputs, gate_grad, 0, 0).astype(BF16)
    grad_up = contract(inputs, up_grad, 0, 0).astype(BF16)
    back_part = contract(gate_grad, gate, 1, 1) + contract(up_grad, up, 1, 1)
    picked_out, picked_back = (
        exchange(
            lax.psum_scatter(rows.astype(BF16), "shard", scatter_dimension=1, tiled=True)
        )[targets].astype(F32)
        for rows in (out_part, back_part)
    )
    combined = jnp.sum((picked_out * weights_flat).reshape(tok_rows, top_count, part), axis=1)
    frame_grad = jnp.sum(picked_back.reshape(tok_rows, top_count, part), axis=1)
    return (
        combined.astype(BF16),
        frame_grad.astype(BF16),
        grad_gate[None],
        grad_up[None],
        grad_down[None],
    )


def per_device(frames, *rest):
    experts, shards = lax.axis_size("expert"), lax.axis_size("shard")
    capacity = 3 * frames.shape[0] // experts
    fits = (
        frames.shape[1] % 128 == 0
        and frames.shape[0] % 128 == 0
        and capacity % 8 == 0
        and experts & (experts - 1) == 0
        and shards & (shards - 1) == 0
    )
    return (fast_device if fits else plain_device)(frames, *rest)


def solution(mesh):
    in_specs = (
        P("expert", "shard"),
        P("expert", None),
        P("expert", None),
        P("expert", "shard"),
        P("expert", None, "shard"),
        P("expert", None, "shard"),
        P("expert", "shard", None),
    )
    out_specs = (
        P("expert", "shard"),
        P("expert", "shard"),
        P("expert", None, "shard"),
        P("expert", None, "shard"),
        P("expert", "shard", None),
    )
    return jax.shard_map(
        per_device, mesh=mesh, in_specs=in_specs, out_specs=out_specs, check_vma=False
    )
```

```python
import functools

import jax
import jax.numpy as jnp
from jax import lax
from jax.experimental import pallas as pl
from jax.experimental.pallas import tpu as pltpu
from jax.sharding import PartitionSpec as P


F32, BF16, I32 = jnp.float32, jnp.bfloat16, jnp.int32
VMEM_LIMIT = 12 * 1024 * 1024


def contract(left, right, left_dim, right_dim):
    return lax.dot_general(
        left, right, (((left_dim,), (right_dim,)), ((), ())), preferred_element_type=F32
    )


def whole_block():
    return pl.BlockSpec(memory_space=pltpu.VMEM)


def scalar_block():
    return pl.BlockSpec(memory_space=pltpu.SMEM)


def selection(me, ids, experts, capacity):
    tok = ids.shape[1]
    expert_of = jnp.bitwise_xor(lax.broadcasted_iota(I32, (experts, tok), 0), me)
    first = ids[0:1, :] == expert_of
    second = ids[1:2, :] == expert_of
    table = jnp.where(first | second, 1.0, 0.0)
    upper = jnp.where(
        lax.broadcasted_iota(I32, (tok, tok), 0) < lax.broadcasted_iota(I32, (tok, tok), 1),
        1.0,
        0.0,
    )
    earlier = contract(table.astype(BF16), upper.astype(BF16), 1, 0).astype(I32)
    slot_first = jnp.where(first, earlier, -1)
    slot_second = jnp.where(second, earlier, -1)

    def one_hot(slots, k):
        rows = lax.broadcasted_iota(I32, (capacity, tok), 0)
        return jnp.where(slots[k : k + 1, :] == rows, 1.0, 0.0).astype(BF16)

    return slot_first, slot_second, one_hot


def dispatch_kernel(me_ref, _, *refs):
    sources, refs = refs[:4], refs[4:]
    send_refs, locals_, sems = refs[:-5], refs[-5:-1], refs[-1]
    copies = [
        pltpu.make_async_copy(source, local, sems.at[i])
        for i, (source, local) in enumerate(zip(sources, locals_))
    ]
    for copy in copies:
        copy.start()
    experts, capacity = len(send_refs), send_refs[0].shape[0]
    ids_ref, gates_ref, frames_ref, cot_ref = locals_
    width = frames_ref.shape[1]
    copies[0].wait()
    slot_first, slot_second, one_hot = selection(me_ref[0], ids_ref[...], experts, capacity)
    for copy in copies[1:]:
        copy.wait()
    gates = jnp.transpose(jnp.concatenate([gates_ref[...]] * 4, axis=0))
    cot = cot_ref[...].astype(F32)
    weighted = jnp.concatenate(
        [(cot * gates[:, 0:1]).astype(BF16), (cot * gates[:, 1:2]).astype(BF16)], axis=0
    )
    frames = frames_ref[...]
    for k in range(experts):
        first, second = one_hot(slot_first, k), one_hot(slot_second, k)
        send_refs[k][:, :width] = contract(first + second, frames, 1, 0).astype(BF16)
        send_refs[k][:, width:] = contract(
            jnp.concatenate([first, second], axis=1), weighted, 1, 0
        ).astype(BF16)


def dispatch(me, place, ids, gates, frames, cot, experts, capacity):
    width = 2 * frames.shape[1]
    sources = (ids, gates, frames, cot)
    return pl.pallas_call(
        dispatch_kernel,
        out_shape=[jax.ShapeDtypeStruct((capacity, width), BF16)] * experts,
        in_specs=[scalar_block()] * 2 + [pl.BlockSpec(memory_space=pltpu.HBM)] * 4,
        out_specs=[whole_block()] * experts,
        scratch_shapes=[pltpu.VMEM(a.shape, a.dtype) for a in sources]
        + [pltpu.SemaphoreType.DMA((4,))],
        compiler_params=pltpu.CompilerParams(vmem_limit_bytes=VMEM_LIMIT),
        name="dispatch",
    )(me, place, *(held(a) for a in sources))


def combine_kernel(me_ref, ids_ref, gates_ref, *refs):
    got_refs, (combined_ref, grad_ref) = refs[:-2], refs[-2:]
    experts = len(got_refs)
    capacity = got_refs[0].shape[0]
    width = combined_ref.shape[1]
    slot_first, slot_second, one_hot = selection(me_ref[0], ids_ref[...], experts, capacity)
    gates = jnp.transpose(jnp.concatenate([gates_ref[...]] * 4, axis=0))
    got = jnp.concatenate([ref[...] for ref in got_refs], axis=0)
    first = jnp.concatenate([one_hot(slot_first, k) for k in range(experts)], axis=0)
    second = jnp.concatenate([one_hot(slot_second, k) for k in range(experts)], axis=0)
    picked = contract(first, got, 0, 0), contract(second, got, 0, 0)
    combined_ref[...] = (
        picked[0][:, :width] * gates[:, 0:1] + picked[1][:, :width] * gates[:, 1:2]
    ).astype(BF16)
    grad_ref[...] = (picked[0][:, width:] + picked[1][:, width:]).astype(BF16)


def combine(me, ids, gates, got):
    tok, width = ids.shape[1], got[0].shape[1] // 2
    return pl.pallas_call(
        combine_kernel,
        out_shape=[jax.ShapeDtypeStruct((tok, width), BF16)] * 2,
        in_specs=[scalar_block()] + [whole_block()] * (2 + len(got)),
        out_specs=[whole_block()] * 2,
        compiler_params=pltpu.CompilerParams(vmem_limit_bytes=VMEM_LIMIT),
        name="combine",
    )(me, ids, gates, *got)


def stacked(refs, axis):
    return jnp.concatenate([ref[...] for ref in refs], axis=axis)


COST = pl.CostEstimate(flops=1 << 20, bytes_accessed=1 << 16, transcendentals=0)


def held(matrix):
    return pltpu.with_memory_space_constraint(matrix, pltpu.HBM)


def call(kernel, shapes, me, arrays, scratch=()):
    return pl.pallas_call(
        kernel,
        out_shape=[jax.ShapeDtypeStruct(shape, BF16) for shape in shapes],
        in_specs=[scalar_block()] + [whole_block()] * len(arrays),
        out_specs=[whole_block()] * len(shapes),
        scratch_shapes=scratch,
        compiler_params=pltpu.CompilerParams(vmem_limit_bytes=VMEM_LIMIT),
        cost_estimate=COST,
    )(me, *arrays)


def prepare_kernel(count, *refs):
    sources, kept, turned, sems = refs[:count], refs[count : 2 * count], refs[2 * count : -1], refs[-1]
    copies = [
        pltpu.make_async_copy(source, target, sems.at[i])
        for i, (source, target) in enumerate(zip(sources, kept))
    ]
    for copy in copies:
        copy.start()
    for copy, source, target in zip(copies, kept, turned):
        copy.wait()

        @pl.loop(0, source.shape[0] // 256)
        def _(i):
            start = pl.multiple_of(i * 256, 256)
            target[:, pl.ds(start, 256)] = jnp.transpose(source[pl.ds(start, 256), :])


def prepare(matrices):
    count = len(matrices)
    shapes = [m.shape for m in matrices] + [m.shape[::-1] for m in matrices]
    return pl.pallas_call(
        functools.partial(prepare_kernel, count),
        out_shape=[jax.ShapeDtypeStruct(shape, BF16) for shape in shapes],
        in_specs=[pl.BlockSpec(memory_space=pltpu.HBM)] * count,
        out_specs=[whole_block()] * (2 * count),
        scratch_shapes=[pltpu.SemaphoreType.DMA((count,))],
        compiler_params=pltpu.CompilerParams(vmem_limit_bytes=VMEM_LIMIT),
        cost_estimate=COST,
    )(*(held(m) for m in matrices))


def ordered(ref, me, count, cut):
    size = ref.shape[0] // count
    starts = [pl.multiple_of(jnp.bitwise_xor(me, j) * size, size) for j in range(count)]
    return jnp.concatenate([ref[pl.ds(start, size), cut] for start in starts], axis=0)


def stack_kernel(me_ref, *refs):
    refs[-1][...] = stacked(refs[:-1], 0)


def stack(me, pieces):
    rows, columns = sum(p.shape[0] for p in pieces), pieces[0].shape[1]
    return call(stack_kernel, [(rows, columns)], me, pieces)[0]


def split_kernel(part, me_ref, *refs):
    whole = stacked(refs[:-2], 0)
    refs[-2][...] = whole[:, :part]
    refs[-1][...] = whole[:, part:]


def split(me, pieces, part):
    rows = sum(p.shape[0] for p in pieces)
    kernel = functools.partial(split_kernel, part)
    return call(kernel, [(rows, part)] * 2, me, pieces)


def forward_kernel(count, part, tile, me_ref, *refs):
    gate_ref, up_ref, hidden_ref, slope_ref, silu_ref, gate_sum, up_sum = refs[count:]
    me = me_ref[0]
    tiles = hidden_ref.shape[1] // tile
    inputs = jnp.concatenate([ref[:, :part] for ref in refs[:count]], axis=1)

    def finish(i):
        cut = slice(i * tile, (i + 1) * tile)
        gate_act, up_act = gate_sum[i % 2], up_sum[i % 2]
        sigma = jax.nn.sigmoid(gate_act)
        silu = gate_act * sigma
        hidden_ref[:, cut] = (silu * up_act).astype(BF16)
        silu_ref[:, cut] = silu.astype(BF16)
        slope_ref[:, cut] = (up_act * sigma * (1.0 + gate_act * (1.0 - sigma))).astype(BF16)

    for i in range(tiles):
        cut = slice(i * tile, (i + 1) * tile)
        gate_sum[i % 2] = contract(inputs, ordered(gate_ref, me, count, cut), 1, 0)
        up_sum[i % 2] = contract(inputs, ordered(up_ref, me, count, cut), 1, 0)
        if i:
            finish(i - 1)
    finish(tiles - 1)


def forward(me, parts, part, gate, up, tile):
    rows, (model, inner) = parts[0].shape[0], gate.shape
    return call(
        functools.partial(forward_kernel, len(parts), part, tile),
        [(rows, inner)] * 3,
        me,
        [*parts, gate, up],
        [pltpu.VMEM((2, rows, tile), F32)] * 2,
    )


def backward_kernel(count, part, tile, me_ref, *refs):
    slope_ref, silu_ref, turned_ref, gate_grad_ref, up_grad_ref, hidden_sum = refs[count:]
    me = me_ref[0]
    tiles = slope_ref.shape[1] // tile
    routed = jnp.concatenate([ref[:, ref.shape[1] - part :] for ref in refs[:count]], axis=1)

    def finish(i):
        cut = slice(i * tile, (i + 1) * tile)
        hidden_grad = hidden_sum[i % 2]
        gate_grad_ref[:, cut] = (hidden_grad * slope_ref[:, cut].astype(F32)).astype(BF16)
        up_grad_ref[:, cut] = (hidden_grad * silu_ref[:, cut].astype(F32)).astype(BF16)

    for i in range(tiles):
        cut = slice(i * tile, (i + 1) * tile)
        hidden_sum[i % 2] = contract(routed, ordered(turned_ref, me, count, cut), 1, 0)
        if i:
            finish(i - 1)
    finish(tiles - 1)


def backward(me, parts, part, down_turned, slope, silu, tile):
    rows, (model, inner) = parts[0].shape[0], down_turned.shape
    return call(
        functools.partial(backward_kernel, len(parts), part, tile),
        [(rows, inner)] * 2,
        me,
        [*parts, slope, silu, down_turned],
        [pltpu.VMEM((2, rows, tile), F32)],
    )


def project_kernel(terms, shards, me_ref, *refs):
    acts, sources, (send_ref, keep_ref) = refs[:terms], refs[terms:-2], refs[-2:]
    part = send_ref.shape[1] // (shards // 2)
    for j in range(shards):
        cut = pl.ds(pl.multiple_of(jnp.bitwise_xor(me_ref[0], j) * part, part), part)
        total = contract(acts[0][...], sources[0][:, cut], 1, 0)
        for t in range(1, terms):
            total = total + contract(acts[t][...], sources[t][:, cut], 1, 0)
        out_ref = send_ref if j % 2 else keep_ref
        out_ref[:, (j // 2) * part : (j // 2 + 1) * part] = total.astype(BF16)


def project(me, acts, matrices, shards):
    rows, model = acts[0].shape[0], matrices[0].shape[1]
    kernel = functools.partial(project_kernel, len(acts), shards)
    return call(kernel, [(rows, model // 2)] * 2, me, [*acts, *matrices])


def weight_in_kernel(count, groups, part, rows, me_ref, *refs):
    frame_refs, refs = refs[: count * groups], refs[count * groups :]
    grad_refs, (gate_hbm, up_hbm, turned_ref, staged, sems) = refs[: 2 * groups], refs[2 * groups :]
    for j in range(count):
        start = pl.multiple_of(jnp.bitwise_xor(me_ref[0], j) * part, part)
        group = frame_refs[j * groups : (j + 1) * groups]
        inputs = jnp.concatenate([ref[:, :part] for ref in group], axis=0)
        turned_ref[pl.ds(start, part), :] = jnp.transpose(inputs)
    blocks, copies = turned_ref.shape[0] // rows, []
    for t, target in enumerate((gate_hbm, up_hbm)):
        for i in range(blocks):
            at = t * blocks + i
            left = turned_ref[i * rows : (i + 1) * rows, :]
            for cut in range(0, staged.shape[2], 256):
                grads = stacked([r.at[:, cut : cut + 256] for r in grad_refs[t * groups : (t + 1) * groups]], 0)
                staged[at, :, cut : cut + 256] = contract(left, grads, 1, 0).astype(BF16)
            copy = pltpu.make_async_copy(
                staged.at[at], target.at[pl.ds(i * rows, rows), :], sems.at[at]
            )
            copy.start()
            copies.append(copy)
    for copy in copies:
        copy.wait()


def weight_down_kernel(count, groups, part, rows, me_ref, *refs):
    cot_refs, hidden_refs = refs[: count * groups], refs[count * groups : -3]
    down_hbm, staged, sems = refs[-3:]
    copies = []
    for i in range(staged.shape[0]):
        cut = slice(i * rows, (i + 1) * rows)
        turned = jnp.transpose(stacked([ref.at[:, cut] for ref in hidden_refs], 0))
        for j in range(count):
            start = pl.multiple_of(jnp.bitwise_xor(me_ref[0], j) * part, part)
            group = cot_refs[j * groups : (j + 1) * groups]
            routed = jnp.concatenate([ref[:, ref.shape[1] - part :] for ref in group], axis=0)
            staged[i, :, pl.ds(start, part)] = contract(turned, routed, 1, 0).astype(BF16)
        copy = pltpu.make_async_copy(staged.at[i], down_hbm.at[pl.ds(i * rows, rows), :], sems.at[i])
        copy.start()
        copies.append(copy)
    for copy in copies:
        copy.wait()


def weight_grads(me, sides, acts, part, shape):
    count, groups = len(sides), len(acts[0])
    inner = acts[0][0].shape[1]
    operands = [a for group in (*sides, *acts) for a in group]
    down = shape[0] == inner and len(acts) == 1
    kernel = weight_down_kernel if down else weight_in_kernel
    rows = 512
    tall = sum(a.shape[0] for a in acts[0])
    blocks = len(acts) * shape[0] // rows
    return pl.pallas_call(
        functools.partial(kernel, count, groups, part, rows),
        out_shape=[jax.ShapeDtypeStruct(shape, BF16)] * len(acts),
        in_specs=[scalar_block()] + [whole_block()] * len(operands),
        out_specs=[pl.BlockSpec(memory_space=pltpu.HBM)] * len(acts),
        scratch_shapes=([] if down else [pltpu.VMEM((shape[0], tall), BF16)])
        + [pltpu.VMEM((blocks, rows, shape[1]), BF16), pltpu.SemaphoreType.DMA((blocks,))],
        compiler_params=pltpu.CompilerParams(vmem_limit_bytes=VMEM_LIMIT),
        cost_estimate=COST,
    )(me, *operands)


def swap(value, axis, bit):
    pairs = [(i, i ^ bit) for i in range(lax.axis_size(axis))]
    return lax.ppermute(value, axis, pairs)


def gathered(own, shards):
    parts, bit = {0: own}, shards // 2
    while bit:
        for j, value in list(parts.items()):
            parts[j ^ bit] = swap(value, "shard", bit)
        bit //= 2
    return [parts[j] for j in range(shards)]


def scattered(send, keep, shards):
    arrived = swap(send, "shard", 1)
    total = (keep.astype(F32) + arrived.astype(F32)).astype(BF16)
    width, bit = total.shape[1], 2
    while bit < shards:
        width //= 2
        sent = swap(total[:, width:], "shard", bit)
        total = (total[:, :width].astype(F32) + sent.astype(F32)).astype(BF16)
        bit *= 2
    return total


def fast_device(frames, expert_ids, gate_weights, cotangent, weight_gate, weight_up, weight_down):
    experts, shards = lax.axis_size("expert"), lax.axis_size("shard")
    tok_rows, part = frames.shape
    capacity = 3 * tok_rows // experts
    expert_at = lax.axis_index("expert").astype(I32).reshape(1)
    me = lax.axis_index("shard").astype(I32).reshape(1)
    ids, gates = expert_ids.T, gate_weights.T
    gate, up, down = weight_gate[0], weight_up[0], weight_down[0]
    tile = 256
    half = experts // 2

    sent = dispatch(expert_at, me, ids, gates, frames, cotangent, experts, capacity)
    got = {0: sent[0]}
    for k in range(1, experts):
        got[k] = swap(sent[k], "expert", k)
    near = stack(me, [got[k] for k in range(half)])
    kept = prepare([gate, up, down])
    gate, up, down, gate_turned, up_turned, down_turned = kept
    far_frames, far_cot = split(me, [got[k] for k in range(half, experts)], part)
    near = gathered(near, shards)
    far_frames = gathered(far_frames, shards)
    far_cot = gathered(far_cot, shards)

    hidden_n, slope_n, silu_n = forward(me, near, part, gate, up, tile)
    hidden_f, slope_f, silu_f = forward(me, far_frames, part, gate, up, tile)
    out_f = project(me, [hidden_f], [down], shards)
    grads_f = backward(me, far_cot, part, down_turned, slope_f, silu_f, tile)
    back_f = project(me, grads_f, [gate_turned, up_turned], shards)
    out_n = project(me, [hidden_n], [down], shards)
    grads_n = backward(me, near, part, down_turned, slope_n, silu_n, tile)
    back_n = project(me, grads_n, [gate_turned, up_turned], shards)
    hidden = [hidden_n, hidden_f]
    gate_grad, up_grad = zip(grads_n, grads_f)
    shape = gate.shape
    (grad_down,) = weight_grads(me, list(zip(near, far_cot)), [hidden], part, shape[::-1])
    grad_gate, grad_up = weight_grads(
        me, list(zip(near, far_frames)), [gate_grad, up_grad], part, shape
    )

    returned = {}
    for far, (out, back) in ((1, (out_f, back_f)), (0, (out_n, back_n))):
        both = jnp.concatenate([scattered(*out, shards), scattered(*back, shards)], axis=1)
        for i in range(half):
            k = far * half + i
            piece = both[i * capacity : (i + 1) * capacity]
            returned[k] = swap(piece, "expert", k) if k else piece
    combined, frame_grad = combine(expert_at, ids, gates, [returned[k] for k in range(experts)])
    return combined, frame_grad, grad_gate[None], grad_up[None], grad_down[None]


def route_slot(flat_ids, experts):
    table = (flat_ids[:, None] == jnp.arange(experts, dtype=jnp.int32)[None, :]).astype(jnp.int32)
    earlier = jnp.cumsum(table, axis=0) - table
    return jnp.sum(earlier * table, axis=1)


def plain_device(frames, expert_ids, gate_weights, cotangent, weight_gate, weight_up, weight_down):
    experts = lax.axis_size("expert")
    tok_rows = frames.shape[0]
    top_count = expert_ids.shape[1]
    capacity = 3 * tok_rows // experts
    total_rows = experts * capacity
    part = frames.shape[1]
    flat_ids = expert_ids.reshape(-1)
    targets = flat_ids * capacity + route_slot(flat_ids, experts)
    weights_flat = gate_weights.reshape(-1, 1)
    gate, up, down = weight_gate[0], weight_up[0], weight_down[0]

    def exchange(values):
        return lax.all_to_all(values, "expert", split_axis=0, concat_axis=0, tiled=True)

    def place_rows(values):
        return jnp.zeros((total_rows, part), values.dtype).at[targets].set(values)

    frame_rows = jnp.repeat(frames, top_count, axis=0)
    cot_rows = jnp.repeat(cotangent, top_count, axis=0).astype(F32) * weights_flat
    inputs, routed = (
        lax.all_gather(exchange(place_rows(rows)), "shard", axis=1, tiled=True)
        for rows in (frame_rows, cot_rows.astype(BF16))
    )
    gate_act, up_act = contract(inputs, gate, 1, 0), contract(inputs, up, 1, 0)
    sigma = jax.nn.sigmoid(gate_act)
    hidden = (gate_act * sigma * up_act).astype(BF16)
    out_part = contract(hidden, down, 1, 0)
    hidden_grad = contract(routed, down, 1, 1)
    grad_down = contract(hidden, routed, 0, 0).astype(BF16)
    gate_grad = (hidden_grad * up_act * sigma * (1.0 + gate_act * (1.0 - sigma))).astype(BF16)
    up_grad = (hidden_grad * gate_act * sigma).astype(BF16)
    grad_gate = contract(inputs, gate_grad, 0, 0).astype(BF16)
    grad_up = contract(inputs, up_grad, 0, 0).astype(BF16)
    back_part = contract(gate_grad, gate, 1, 1) + contract(up_grad, up, 1, 1)
    picked_out, picked_back = (
        exchange(
            lax.psum_scatter(rows.astype(BF16), "shard", scatter_dimension=1, tiled=True)
        )[targets].astype(F32)
        for rows in (out_part, back_part)
    )
    combined = jnp.sum((picked_out * weights_flat).reshape(tok_rows, top_count, part), axis=1)
    frame_grad = jnp.sum(picked_back.reshape(tok_rows, top_count, part), axis=1)
    return (
        combined.astype(BF16),
        frame_grad.astype(BF16),
        grad_gate[None],
        grad_up[None],
        grad_down[None],
    )


def per_device(frames, *rest):
    experts, shards = lax.axis_size("expert"), lax.axis_size("shard")
    capacity = 3 * frames.shape[0] // experts
    fits = (
        frames.shape[1] % 128 == 0
        and frames.shape[0] % 128 == 0
        and capacity % 8 == 0
        and experts & (experts - 1) == 0
        and shards & (shards - 1) == 0
    )
    return (fast_device if fits else plain_device)(frames, *rest)


def solution(mesh):
    in_specs = (
        P("expert", "shard"),
        P("expert", None),
        P("expert", None),
        P("expert", "shard"),
        P("expert", None, "shard"),
        P("expert", None, "shard"),
        P("expert", "shard", None),
    )
    out_specs = (
        P("expert", "shard"),
        P("expert", "shard"),
        P("expert", None, "shard"),
        P("expert", None, "shard"),
        P("expert", "shard", None),
    )
    return jax.shard_map(
        per_device, mesh=mesh, in_specs=in_specs, out_specs=out_specs, check_vma=False
    )
```

```python
import functools

import jax
import jax.numpy as jnp
from jax import lax
from jax.experimental import pallas as pl
from jax.experimental.pallas import tpu as pltpu
from jax.sharding import PartitionSpec as P


F32, BF16, I32 = jnp.float32, jnp.bfloat16, jnp.int32
VMEM_LIMIT = 12 * 1024 * 1024


def contract(left, right, left_dim, right_dim):
    return lax.dot_general(
        left, right, (((left_dim,), (right_dim,)), ((), ())), preferred_element_type=F32
    )


def whole_block():
    return pl.BlockSpec(memory_space=pltpu.VMEM)


def scalar_block():
    return pl.BlockSpec(memory_space=pltpu.SMEM)


def selection(me, ids, experts, capacity):
    tok = ids.shape[1]
    expert_of = jnp.bitwise_xor(lax.broadcasted_iota(I32, (experts, tok), 0), me)
    first = ids[0:1, :] == expert_of
    second = ids[1:2, :] == expert_of
    table = jnp.where(first | second, 1.0, 0.0)
    upper = jnp.where(
        lax.broadcasted_iota(I32, (tok, tok), 0) < lax.broadcasted_iota(I32, (tok, tok), 1),
        1.0,
        0.0,
    )
    earlier = contract(table.astype(BF16), upper.astype(BF16), 1, 0).astype(I32)
    slot_first = jnp.where(first, earlier, -1)
    slot_second = jnp.where(second, earlier, -1)

    def one_hot(slots, k):
        rows = lax.broadcasted_iota(I32, (capacity, tok), 0)
        return jnp.where(slots[k : k + 1, :] == rows, 1.0, 0.0).astype(BF16)

    return slot_first, slot_second, one_hot


def dispatch_kernel(me_ref, _, *refs):
    sources, refs = refs[:4], refs[4:]
    send_refs, locals_, sems = refs[:-5], refs[-5:-1], refs[-1]
    copies = [
        pltpu.make_async_copy(source, local, sems.at[i])
        for i, (source, local) in enumerate(zip(sources, locals_))
    ]
    for copy in copies:
        copy.start()
    experts, capacity = len(send_refs), send_refs[0].shape[0]
    ids_ref, gates_ref, frames_ref, cot_ref = locals_
    width = frames_ref.shape[1]
    copies[0].wait()
    slot_first, slot_second, one_hot = selection(me_ref[0], ids_ref[...], experts, capacity)
    for copy in copies[1:]:
        copy.wait()
    gates = jnp.transpose(jnp.concatenate([gates_ref[...]] * 4, axis=0))
    cot = cot_ref[...].astype(F32)
    weighted = jnp.concatenate(
        [(cot * gates[:, 0:1]).astype(BF16), (cot * gates[:, 1:2]).astype(BF16)], axis=0
    )
    frames = frames_ref[...]
    for k in range(experts):
        first, second = one_hot(slot_first, k), one_hot(slot_second, k)
        send_refs[k][:, :width] = contract(first + second, frames, 1, 0).astype(BF16)
        send_refs[k][:, width:] = contract(
            jnp.concatenate([first, second], axis=1), weighted, 1, 0
        ).astype(BF16)


def dispatch(me, place, ids, gates, frames, cot, experts, capacity):
    width = 2 * frames.shape[1]
    sources = (ids, gates, frames, cot)
    return pl.pallas_call(
        dispatch_kernel,
        out_shape=[jax.ShapeDtypeStruct((capacity, width), BF16)] * experts,
        in_specs=[scalar_block()] * 2 + [pl.BlockSpec(memory_space=pltpu.HBM)] * 4,
        out_specs=[whole_block()] * experts,
        scratch_shapes=[pltpu.VMEM(a.shape, a.dtype) for a in sources]
        + [pltpu.SemaphoreType.DMA((4,))],
        compiler_params=pltpu.CompilerParams(vmem_limit_bytes=VMEM_LIMIT),
        name="dispatch",
    )(me, place, *(held(a) for a in sources))


def select_kernel(experts, me_ref, ids_ref, *turned_refs):
    capacity = turned_refs[0].shape[1] // experts
    *slots, one_hot = selection(me_ref[0], ids_ref[...], experts, capacity)
    for slot, turned_ref in zip(slots, turned_refs):
        rows = jnp.concatenate([one_hot(slot, k) for k in range(experts)], axis=0)
        turned_ref[...] = jnp.transpose(rows)


def select(me, ids, experts, capacity):
    kernel = functools.partial(select_kernel, experts)
    return call(kernel, [(ids.shape[1], experts * capacity)] * 2, me, [ids])


def combine_kernel(_, first_ref, second_ref, gates_ref, *refs):
    got_refs, (combined_ref, grad_ref) = refs[:-2], refs[-2:]
    width = combined_ref.shape[1]
    gates = jnp.transpose(jnp.concatenate([gates_ref[...]] * 4, axis=0))
    got = stacked(got_refs, 0)
    first = contract(first_ref[...], got, 1, 0)
    second = contract(second_ref[...], got, 1, 0)
    combined_ref[...] = (
        first[:, :width] * gates[:, 0:1] + second[:, :width] * gates[:, 1:2]
    ).astype(BF16)
    grad_ref[...] = (first[:, width:] + second[:, width:]).astype(BF16)


def combine(me, picks, gates, got):
    shape = (gates.shape[1], got[0].shape[1] // 2)
    return call(combine_kernel, [shape] * 2, me, [*picks, gates, *got])


def stacked(refs, axis):
    return jnp.concatenate([ref[...] for ref in refs], axis=axis)


COST = pl.CostEstimate(flops=1 << 20, bytes_accessed=1 << 16, transcendentals=0)


def held(matrix):
    return pltpu.with_memory_space_constraint(matrix, pltpu.HBM)


def call(kernel, shapes, me, arrays, scratch=()):
    return pl.pallas_call(
        kernel,
        out_shape=[jax.ShapeDtypeStruct(shape, BF16) for shape in shapes],
        in_specs=[scalar_block()] + [whole_block()] * len(arrays),
        out_specs=[whole_block()] * len(shapes),
        scratch_shapes=scratch,
        compiler_params=pltpu.CompilerParams(vmem_limit_bytes=VMEM_LIMIT),
        cost_estimate=COST,
    )(me, *arrays)


def prepare_kernel(count, *refs):
    sources, kept, turned, sems = refs[:count], refs[count : 2 * count], refs[2 * count : -1], refs[-1]
    copies = [
        pltpu.make_async_copy(source, target, sems.at[i])
        for i, (source, target) in enumerate(zip(sources, kept))
    ]
    for copy in copies:
        copy.start()
    for copy, source, target in zip(copies, kept, turned):
        copy.wait()

        @pl.loop(0, source.shape[0] // 256)
        def _(i):
            start = pl.multiple_of(i * 256, 256)
            target[:, pl.ds(start, 256)] = jnp.transpose(source[pl.ds(start, 256), :])


def prepare(matrices):
    count = len(matrices)
    shapes = [m.shape for m in matrices] + [m.shape[::-1] for m in matrices]
    return pl.pallas_call(
        functools.partial(prepare_kernel, count),
        out_shape=[jax.ShapeDtypeStruct(shape, BF16) for shape in shapes],
        in_specs=[pl.BlockSpec(memory_space=pltpu.HBM)] * count,
        out_specs=[whole_block()] * (2 * count),
        scratch_shapes=[pltpu.SemaphoreType.DMA((count,))],
        compiler_params=pltpu.CompilerParams(vmem_limit_bytes=VMEM_LIMIT),
        cost_estimate=COST,
    )(*(held(m) for m in matrices))


def ordered(ref, me, count, cut):
    size = ref.shape[0] // count
    starts = [pl.multiple_of(jnp.bitwise_xor(me, j) * size, size) for j in range(count)]
    return jnp.concatenate([ref[pl.ds(start, size), cut] for start in starts], axis=0)


def split_kernel(part, me_ref, *refs):
    whole = stacked(refs[:-2], 0)
    refs[-2][...] = whole[:, :part]
    refs[-1][...] = whole[:, part:]


def split(me, pieces, part):
    rows = sum(p.shape[0] for p in pieces)
    kernel = functools.partial(split_kernel, part)
    return call(kernel, [(rows, part)] * 2, me, pieces)


def forward_kernel(count, part, tile, me_ref, *refs):
    gate_ref, up_ref, hidden_ref, slope_ref, silu_ref, gate_sum, up_sum = refs[count:]
    me = me_ref[0]
    tiles = hidden_ref.shape[1] // tile
    inputs = jnp.concatenate([ref[:, :part] for ref in refs[:count]], axis=1)

    def finish(i):
        cut = slice(i * tile, (i + 1) * tile)
        gate_act, up_act = gate_sum[i % 2], up_sum[i % 2]
        sigma = jax.nn.sigmoid(gate_act)
        silu = gate_act * sigma
        hidden_ref[:, cut] = (silu * up_act).astype(BF16)
        silu_ref[:, cut] = silu.astype(BF16)
        slope_ref[:, cut] = (up_act * sigma * (1.0 + gate_act * (1.0 - sigma))).astype(BF16)

    for i in range(tiles):
        cut = slice(i * tile, (i + 1) * tile)
        gate_sum[i % 2] = contract(inputs, ordered(gate_ref, me, count, cut), 1, 0)
        up_sum[i % 2] = contract(inputs, ordered(up_ref, me, count, cut), 1, 0)
        if i:
            finish(i - 1)
    finish(tiles - 1)


def forward(me, parts, part, gate, up, tile):
    rows, (model, inner) = parts[0].shape[0], gate.shape
    return call(
        functools.partial(forward_kernel, len(parts), part, tile),
        [(rows, inner)] * 3,
        me,
        [*parts, gate, up],
        [pltpu.VMEM((2, rows, tile), F32)] * 2,
    )


def backward_kernel(count, part, tile, me_ref, *refs):
    slope_ref, silu_ref, turned_ref, gate_grad_ref, up_grad_ref, hidden_sum = refs[count:]
    me = me_ref[0]
    tiles = slope_ref.shape[1] // tile
    routed = jnp.concatenate([ref[:, ref.shape[1] - part :] for ref in refs[:count]], axis=1)

    def finish(i):
        cut = slice(i * tile, (i + 1) * tile)
        hidden_grad = hidden_sum[i % 2]
        gate_grad_ref[:, cut] = (hidden_grad * slope_ref[:, cut].astype(F32)).astype(BF16)
        up_grad_ref[:, cut] = (hidden_grad * silu_ref[:, cut].astype(F32)).astype(BF16)

    for i in range(tiles):
        cut = slice(i * tile, (i + 1) * tile)
        hidden_sum[i % 2] = contract(routed, ordered(turned_ref, me, count, cut), 1, 0)
        if i:
            finish(i - 1)
    finish(tiles - 1)


def backward(me, parts, part, down_turned, slope, silu, tile):
    rows, (model, inner) = parts[0].shape[0], down_turned.shape
    return call(
        functools.partial(backward_kernel, len(parts), part, tile),
        [(rows, inner)] * 2,
        me,
        [*parts, slope, silu, down_turned],
        [pltpu.VMEM((2, rows, tile), F32)],
    )


def project_kernel(terms, shards, sides, me_ref, *refs):
    acts, sources, out_refs = refs[:terms], refs[terms : 2 * terms], refs[2 * terms :]
    part = sources[0].shape[1] // shards
    for side, out_ref in zip(sides, out_refs):
        for i in range(shards // 2):
            start = pl.multiple_of(jnp.bitwise_xor(me_ref[0], 2 * i + side) * part, part)
            cut = pl.ds(start, part)
            total = contract(acts[0][...], sources[0][:, cut], 1, 0)
            for t in range(1, terms):
                total = total + contract(acts[t][...], sources[t][:, cut], 1, 0)
            out_ref[:, i * part : (i + 1) * part] = total.astype(BF16)


def project(me, acts, matrices, shards, sides):
    rows, model = acts[0].shape[0], matrices[0].shape[1]
    kernel = functools.partial(project_kernel, len(acts), shards, sides)
    return call(kernel, [(rows, model // 2)] * len(sides), me, [*acts, *matrices])


def weight_in_kernel(count, groups, part, rows, me_ref, *refs):
    frame_refs, refs = refs[: count * groups], refs[count * groups :]
    grad_refs, (gate_hbm, up_hbm, turned_ref, staged, sems) = refs[: 2 * groups], refs[2 * groups :]
    for j in range(count):
        start = pl.multiple_of(jnp.bitwise_xor(me_ref[0], j) * part, part)
        group = frame_refs[j * groups : (j + 1) * groups]
        inputs = jnp.concatenate([ref[:, :part] for ref in group], axis=0)
        turned_ref[pl.ds(start, part), :] = jnp.transpose(inputs)
    blocks, copies = turned_ref.shape[0] // rows, []
    for t, target in enumerate((gate_hbm, up_hbm)):
        for i in range(blocks):
            at = t * blocks + i
            left = turned_ref[i * rows : (i + 1) * rows, :]
            for cut in range(0, staged.shape[2], 256):
                grads = stacked([r.at[:, cut : cut + 256] for r in grad_refs[t * groups : (t + 1) * groups]], 0)
                staged[at, :, cut : cut + 256] = contract(left, grads, 1, 0).astype(BF16)
            copy = pltpu.make_async_copy(
                staged.at[at], target.at[pl.ds(i * rows, rows), :], sems.at[at]
            )
            copy.start()
            copies.append(copy)
    for copy in copies:
        copy.wait()


def weight_down_kernel(count, groups, part, rows, me_ref, *refs):
    cot_refs, hidden_refs = refs[: count * groups], refs[count * groups : -3]
    down_hbm, staged, sems = refs[-3:]
    copies = []
    for i in range(staged.shape[0]):
        cut = slice(i * rows, (i + 1) * rows)
        turned = jnp.transpose(stacked([ref.at[:, cut] for ref in hidden_refs], 0))
        for j in range(count):
            start = pl.multiple_of(jnp.bitwise_xor(me_ref[0], j) * part, part)
            group = cot_refs[j * groups : (j + 1) * groups]
            routed = jnp.concatenate([ref[:, ref.shape[1] - part :] for ref in group], axis=0)
            staged[i, :, pl.ds(start, part)] = contract(turned, routed, 1, 0).astype(BF16)
        copy = pltpu.make_async_copy(staged.at[i], down_hbm.at[pl.ds(i * rows, rows), :], sems.at[i])
        copy.start()
        copies.append(copy)
    for copy in copies:
        copy.wait()


def weight_grads(me, sides, acts, part, shape):
    count, groups = len(sides), len(acts[0])
    inner = acts[0][0].shape[1]
    operands = [a for group in (*sides, *acts) for a in group]
    down = shape[0] == inner and len(acts) == 1
    kernel = weight_down_kernel if down else weight_in_kernel
    rows = 512
    tall = sum(a.shape[0] for a in acts[0])
    blocks = len(acts) * shape[0] // rows
    return pl.pallas_call(
        functools.partial(kernel, count, groups, part, rows),
        out_shape=[jax.ShapeDtypeStruct(shape, BF16)] * len(acts),
        in_specs=[scalar_block()] + [whole_block()] * len(operands),
        out_specs=[pl.BlockSpec(memory_space=pltpu.HBM)] * len(acts),
        scratch_shapes=([] if down else [pltpu.VMEM((shape[0], tall), BF16)])
        + [pltpu.VMEM((blocks, rows, shape[1]), BF16), pltpu.SemaphoreType.DMA((blocks,))],
        compiler_params=pltpu.CompilerParams(vmem_limit_bytes=VMEM_LIMIT),
        cost_estimate=COST,
    )(me, *operands)


def swap(value, axis, bit):
    pairs = [(i, i ^ bit) for i in range(lax.axis_size(axis))]
    return lax.ppermute(value, axis, pairs)


def gathered(own, shards):
    parts, bit = {0: own}, shards // 2
    while bit:
        for j, value in list(parts.items()):
            parts[j ^ bit] = swap(value, "shard", bit)
        bit //= 2
    return [parts[j] for j in range(shards)]


def scattered(send, keep, shards):
    arrived = swap(send, "shard", 1)
    total = (keep.astype(F32) + arrived.astype(F32)).astype(BF16)
    width, bit = total.shape[1], 2
    while bit < shards:
        width //= 2
        sent = swap(total[:, width:], "shard", bit)
        total = (total[:, :width].astype(F32) + sent.astype(F32)).astype(BF16)
        bit *= 2
    return total


def fast_device(frames, expert_ids, gate_weights, cotangent, weight_gate, weight_up, weight_down):
    experts, shards = lax.axis_size("expert"), lax.axis_size("shard")
    tok_rows, part = frames.shape
    capacity = 3 * tok_rows // experts
    expert_at = lax.axis_index("expert").astype(I32).reshape(1)
    me = lax.axis_index("shard").astype(I32).reshape(1)
    ids, gates = expert_ids.T, gate_weights.T
    gate, up, down = weight_gate[0], weight_up[0], weight_down[0]
    tile = 256
    half = experts // 2

    sent = dispatch(expert_at, me, ids, gates, frames, cotangent, experts, capacity)
    got = {0: sent[0]}
    for k in range(1, experts):
        got[k] = swap(sent[k], "expert", k)
    near_frames, near_cot = split(me, [got[k] for k in range(half)], part)
    picks = select(expert_at, ids, experts, capacity)
    kept = prepare([gate, up, down])
    gate, up, down, gate_turned, up_turned, down_turned = kept
    far_frames, far_cot = split(me, [got[k] for k in range(half, experts)], part)
    near_frames, near_cot = gathered(near_frames, shards), gathered(near_cot, shards)
    far_frames, far_cot = gathered(far_frames, shards), gathered(far_cot, shards)

    hidden_n, slope_n, silu_n = forward(me, near_frames, part, gate, up, tile)
    hidden_f, slope_f, silu_f = forward(me, far_frames, part, gate, up, tile)
    out_f = project(me, [hidden_f], [down], shards, (1, 0))
    grads_f = backward(me, far_cot, part, down_turned, slope_f, silu_f, tile)
    turned = [gate_turned, up_turned]
    back_f = [
        *project(me, grads_f, turned, shards, (1,)), *project(me, grads_f, turned, shards, (0,))
    ]
    out_n = project(me, [hidden_n], [down], shards, (1, 0))
    grads_n = backward(me, near_cot, part, down_turned, slope_n, silu_n, tile)
    back_n = [
        *project(me, grads_n, turned, shards, (1,)), *project(me, grads_n, turned, shards, (0,))
    ]
    hidden = [hidden_n, hidden_f]
    gate_grad, up_grad = zip(grads_n, grads_f)
    shape = gate.shape
    (grad_down,) = weight_grads(me, list(zip(near_cot, far_cot)), [hidden], part, shape[::-1])
    grad_gate, grad_up = weight_grads(
        me, list(zip(near_frames, far_frames)), [gate_grad, up_grad], part, shape
    )

    returned = {}
    for far, (out, back) in ((1, (out_f, back_f)), (0, (out_n, back_n))):
        both = jnp.concatenate([scattered(*out, shards), scattered(*back, shards)], axis=1)
        for i in range(half):
            k = far * half + i
            piece = both[i * capacity : (i + 1) * capacity]
            returned[k] = swap(piece, "expert", k) if k else piece
    combined, frame_grad = combine(me, picks, gates, [returned[k] for k in range(experts)])
    return combined, frame_grad, grad_gate[None], grad_up[None], grad_down[None]


def route_slot(flat_ids, experts):
    table = (flat_ids[:, None] == jnp.arange(experts, dtype=jnp.int32)[None, :]).astype(jnp.int32)
    earlier = jnp.cumsum(table, axis=0) - table
    return jnp.sum(earlier * table, axis=1)


def plain_device(frames, expert_ids, gate_weights, cotangent, weight_gate, weight_up, weight_down):
    experts = lax.axis_size("expert")
    tok_rows = frames.shape[0]
    top_count = expert_ids.shape[1]
    capacity = 3 * tok_rows // experts
    total_rows = experts * capacity
    part = frames.shape[1]
    flat_ids = expert_ids.reshape(-1)
    targets = flat_ids * capacity + route_slot(flat_ids, experts)
    weights_flat = gate_weights.reshape(-1, 1)
    gate, up, down = weight_gate[0], weight_up[0], weight_down[0]

    def exchange(values):
        return lax.all_to_all(values, "expert", split_axis=0, concat_axis=0, tiled=True)

    def place_rows(values):
        return jnp.zeros((total_rows, part), values.dtype).at[targets].set(values)

    frame_rows = jnp.repeat(frames, top_count, axis=0)
    cot_rows = jnp.repeat(cotangent, top_count, axis=0).astype(F32) * weights_flat
    inputs, routed = (
        lax.all_gather(exchange(place_rows(rows)), "shard", axis=1, tiled=True)
        for rows in (frame_rows, cot_rows.astype(BF16))
    )
    gate_act, up_act = contract(inputs, gate, 1, 0), contract(inputs, up, 1, 0)
    sigma = jax.nn.sigmoid(gate_act)
    hidden = (gate_act * sigma * up_act).astype(BF16)
    out_part = contract(hidden, down, 1, 0)
    hidden_grad = contract(routed, down, 1, 1)
    grad_down = contract(hidden, routed, 0, 0).astype(BF16)
    gate_grad = (hidden_grad * up_act * sigma * (1.0 + gate_act * (1.0 - sigma))).astype(BF16)
    up_grad = (hidden_grad * gate_act * sigma).astype(BF16)
    grad_gate = contract(inputs, gate_grad, 0, 0).astype(BF16)
    grad_up = contract(inputs, up_grad, 0, 0).astype(BF16)
    back_part = contract(gate_grad, gate, 1, 1) + contract(up_grad, up, 1, 1)
    picked_out, picked_back = (
        exchange(
            lax.psum_scatter(rows.astype(BF16), "shard", scatter_dimension=1, tiled=True)
        )[targets].astype(F32)
        for rows in (out_part, back_part)
    )
    combined = jnp.sum((picked_out * weights_flat).reshape(tok_rows, top_count, part), axis=1)
    frame_grad = jnp.sum(picked_back.reshape(tok_rows, top_count, part), axis=1)
    return (
        combined.astype(BF16),
        frame_grad.astype(BF16),
        grad_gate[None],
        grad_up[None],
        grad_down[None],
    )


def per_device(frames, *rest):
    experts, shards = lax.axis_size("expert"), lax.axis_size("shard")
    capacity = 3 * frames.shape[0] // experts
    fits = (
        frames.shape[1] % 128 == 0
        and frames.shape[0] % 128 == 0
        and capacity % 8 == 0
        and experts & (experts - 1) == 0
        and shards & (shards - 1) == 0
    )
    return (fast_device if fits else plain_device)(frames, *rest)


def solution(mesh):
    in_specs = (
        P("expert", "shard"),
        P("expert", None),
        P("expert", None),
        P("expert", "shard"),
        P("expert", None, "shard"),
        P("expert", None, "shard"),
        P("expert", "shard", None),
    )
    out_specs = (
        P("expert", "shard"),
        P("expert", "shard"),
        P("expert", None, "shard"),
        P("expert", None, "shard"),
        P("expert", "shard", None),
    )
    return jax.shard_map(
        per_device, mesh=mesh, in_specs=in_specs, out_specs=out_specs, check_vma=False
    )
```

```python
import functools

import jax
import jax.numpy as jnp
from jax import lax
from jax.experimental import pallas as pl
from jax.experimental.pallas import tpu as pltpu
from jax.sharding import PartitionSpec as P


F32, BF16, I32 = jnp.float32, jnp.bfloat16, jnp.int32
VMEM_LIMIT = 12 * 1024 * 1024


def contract(left, right, left_dim, right_dim):
    return lax.dot_general(
        left, right, (((left_dim,), (right_dim,)), ((), ())), preferred_element_type=F32
    )


def whole_block():
    return pl.BlockSpec(memory_space=pltpu.VMEM)


def scalar_block():
    return pl.BlockSpec(memory_space=pltpu.SMEM)


def selection(me, ids, experts, capacity):
    tok = ids.shape[1]
    expert_of = jnp.bitwise_xor(lax.broadcasted_iota(I32, (experts, tok), 0), me)
    first = ids[0:1, :] == expert_of
    second = ids[1:2, :] == expert_of
    table = jnp.where(first | second, 1.0, 0.0)
    upper = jnp.where(
        lax.broadcasted_iota(I32, (tok, tok), 0) < lax.broadcasted_iota(I32, (tok, tok), 1),
        1.0,
        0.0,
    )
    earlier = contract(table.astype(BF16), upper.astype(BF16), 1, 0).astype(I32)
    slot_first = jnp.where(first, earlier, -1)
    slot_second = jnp.where(second, earlier, -1)

    def one_hot(slots, k):
        rows = lax.broadcasted_iota(I32, (capacity, tok), 0)
        return jnp.where(slots[k : k + 1, :] == rows, 1.0, 0.0).astype(BF16)

    return slot_first, slot_second, one_hot


def dispatch_kernel(me_ref, _, *refs):
    sources, refs = refs[:4], refs[4:]
    send_refs, locals_, sems = refs[:-5], refs[-5:-1], refs[-1]
    copies = [
        pltpu.make_async_copy(source, local, sems.at[i])
        for i, (source, local) in enumerate(zip(sources, locals_))
    ]
    for copy in copies:
        copy.start()
    experts, capacity = len(send_refs), send_refs[0].shape[0]
    ids_ref, gates_ref, frames_ref, cot_ref = locals_
    width = frames_ref.shape[1]
    copies[0].wait()
    slot_first, slot_second, one_hot = selection(me_ref[0], ids_ref[...], experts, capacity)
    for copy in copies[1:]:
        copy.wait()
    gates = jnp.transpose(jnp.concatenate([gates_ref[...]] * 4, axis=0))
    cot = cot_ref[...].astype(F32)
    weighted = jnp.concatenate(
        [(cot * gates[:, 0:1]).astype(BF16), (cot * gates[:, 1:2]).astype(BF16)], axis=0
    )
    frames = frames_ref[...]
    for k in range(experts):
        first, second = one_hot(slot_first, k), one_hot(slot_second, k)
        send_refs[k][:, :width] = contract(first + second, frames, 1, 0).astype(BF16)
        send_refs[k][:, width:] = contract(
            jnp.concatenate([first, second], axis=1), weighted, 1, 0
        ).astype(BF16)


def dispatch(me, place, ids, gates, frames, cot, experts, capacity):
    width = 2 * frames.shape[1]
    sources = (ids, gates, frames, cot)
    return pl.pallas_call(
        dispatch_kernel,
        out_shape=[jax.ShapeDtypeStruct((capacity, width), BF16)] * experts,
        in_specs=[scalar_block()] * 2 + [pl.BlockSpec(memory_space=pltpu.HBM)] * 4,
        out_specs=[whole_block()] * experts,
        scratch_shapes=[pltpu.VMEM(a.shape, a.dtype) for a in sources]
        + [pltpu.SemaphoreType.DMA((4,))],
        compiler_params=pltpu.CompilerParams(vmem_limit_bytes=VMEM_LIMIT),
        name="dispatch",
    )(me, place, *(held(a) for a in sources))


def select_kernel(experts, me_ref, ids_ref, *turned_refs):
    capacity = turned_refs[0].shape[1] // experts
    *slots, one_hot = selection(me_ref[0], ids_ref[...], experts, capacity)
    for slot, turned_ref in zip(slots, turned_refs):
        rows = jnp.concatenate([one_hot(slot, k) for k in range(experts)], axis=0)
        turned_ref[...] = jnp.transpose(rows)


def select(me, ids, experts, capacity):
    kernel = functools.partial(select_kernel, experts)
    return call(kernel, [(ids.shape[1], experts * capacity)] * 2, me, [ids])


def combine_kernel(_, first_ref, second_ref, gates_ref, *refs):
    got_refs, (combined_ref, grad_ref) = refs[:-2], refs[-2:]
    width = combined_ref.shape[1]
    gates = jnp.transpose(jnp.concatenate([gates_ref[...]] * 4, axis=0))
    got = stacked(got_refs, 0)
    first = contract(first_ref[...], got, 1, 0)
    second = contract(second_ref[...], got, 1, 0)
    combined_ref[...] = (
        first[:, :width] * gates[:, 0:1] + second[:, :width] * gates[:, 1:2]
    ).astype(BF16)
    grad_ref[...] = (first[:, width:] + second[:, width:]).astype(BF16)


def combine(me, picks, gates, got):
    shape = (gates.shape[1], got[0].shape[1] // 2)
    return call(combine_kernel, [shape] * 2, me, [*picks, gates, *got])


def stacked(refs, axis):
    return jnp.concatenate([ref[...] for ref in refs], axis=axis)


COST = pl.CostEstimate(flops=1 << 20, bytes_accessed=1 << 16, transcendentals=0)


def held(matrix):
    return pltpu.with_memory_space_constraint(matrix, pltpu.HBM)


def call(kernel, shapes, me, arrays, scratch=()):
    return pl.pallas_call(
        kernel,
        out_shape=[jax.ShapeDtypeStruct(shape, BF16) for shape in shapes],
        in_specs=[scalar_block()] + [whole_block()] * len(arrays),
        out_specs=[whole_block()] * len(shapes),
        scratch_shapes=scratch,
        compiler_params=pltpu.CompilerParams(vmem_limit_bytes=VMEM_LIMIT),
        cost_estimate=COST,
    )(me, *arrays)


def prepare_kernel(count, *refs):
    sources, kept, turned, sems = refs[:count], refs[count : 2 * count], refs[2 * count : -1], refs[-1]
    copies = [
        pltpu.make_async_copy(source, target, sems.at[i])
        for i, (source, target) in enumerate(zip(sources, kept))
    ]
    for copy in copies:
        copy.start()
    for copy, source, target in zip(copies, kept, turned):
        copy.wait()

        @pl.loop(0, source.shape[0] // 256)
        def _(i):
            start = pl.multiple_of(i * 256, 256)
            target[:, pl.ds(start, 256)] = jnp.transpose(source[pl.ds(start, 256), :])


def prepare(matrices):
    count = len(matrices)
    shapes = [m.shape for m in matrices] + [m.shape[::-1] for m in matrices]
    return pl.pallas_call(
        functools.partial(prepare_kernel, count),
        out_shape=[jax.ShapeDtypeStruct(shape, BF16) for shape in shapes],
        in_specs=[pl.BlockSpec(memory_space=pltpu.HBM)] * count,
        out_specs=[whole_block()] * (2 * count),
        scratch_shapes=[pltpu.SemaphoreType.DMA((count,))],
        compiler_params=pltpu.CompilerParams(vmem_limit_bytes=VMEM_LIMIT),
        cost_estimate=COST,
    )(*(held(m) for m in matrices))


def ordered(ref, me, count, cut):
    size = ref.shape[0] // count
    starts = [pl.multiple_of(jnp.bitwise_xor(me, j) * size, size) for j in range(count)]
    return jnp.concatenate([ref[pl.ds(start, size), cut] for start in starts], axis=0)


def split_kernel(part, me_ref, *refs):
    whole = stacked(refs[:-2], 0)
    refs[-2][...] = whole[:, :part]
    refs[-1][...] = whole[:, part:]


def split(me, pieces, part):
    rows = sum(p.shape[0] for p in pieces)
    kernel = functools.partial(split_kernel, part)
    return call(kernel, [(rows, part)] * 2, me, pieces)


def forward_kernel(count, part, tile, me_ref, *refs):
    gate_ref, up_ref, hidden_ref, slope_ref, silu_ref, gate_sum, up_sum = refs[count:]
    me = me_ref[0]
    tiles = hidden_ref.shape[1] // tile
    inputs = jnp.concatenate([ref[:, :part] for ref in refs[:count]], axis=1)

    def finish(i):
        cut = slice(i * tile, (i + 1) * tile)
        gate_act, up_act = gate_sum[i % 2], up_sum[i % 2]
        sigma = jax.nn.sigmoid(gate_act)
        silu = gate_act * sigma
        hidden_ref[:, cut] = (silu * up_act).astype(BF16)
        silu_ref[:, cut] = silu.astype(BF16)
        slope_ref[:, cut] = (up_act * sigma * (1.0 + gate_act * (1.0 - sigma))).astype(BF16)

    for i in range(tiles):
        cut = slice(i * tile, (i + 1) * tile)
        gate_sum[i % 2] = contract(inputs, ordered(gate_ref, me, count, cut), 1, 0)
        up_sum[i % 2] = contract(inputs, ordered(up_ref, me, count, cut), 1, 0)
        if i:
            finish(i - 1)
    finish(tiles - 1)


def forward(me, parts, part, gate, up, tile):
    rows, (model, inner) = parts[0].shape[0], gate.shape
    return call(
        functools.partial(forward_kernel, len(parts), part, tile),
        [(rows, inner)] * 3,
        me,
        [*parts, gate, up],
        [pltpu.VMEM((2, rows, tile), F32)] * 2,
    )


def backward_kernel(count, part, tile, me_ref, *refs):
    slope_ref, silu_ref, turned_ref, gate_grad_ref, up_grad_ref, hidden_sum = refs[count:]
    me = me_ref[0]
    tiles = slope_ref.shape[1] // tile
    routed = jnp.concatenate([ref[:, ref.shape[1] - part :] for ref in refs[:count]], axis=1)

    def finish(i):
        cut = slice(i * tile, (i + 1) * tile)
        hidden_grad = hidden_sum[i % 2]
        gate_grad_ref[:, cut] = (hidden_grad * slope_ref[:, cut].astype(F32)).astype(BF16)
        up_grad_ref[:, cut] = (hidden_grad * silu_ref[:, cut].astype(F32)).astype(BF16)

    for i in range(tiles):
        cut = slice(i * tile, (i + 1) * tile)
        hidden_sum[i % 2] = contract(routed, ordered(turned_ref, me, count, cut), 1, 0)
        if i:
            finish(i - 1)
    finish(tiles - 1)


def backward(me, parts, part, down_turned, slope, silu, tile):
    rows, (model, inner) = parts[0].shape[0], down_turned.shape
    return call(
        functools.partial(backward_kernel, len(parts), part, tile),
        [(rows, inner)] * 2,
        me,
        [*parts, slope, silu, down_turned],
        [pltpu.VMEM((2, rows, tile), F32)],
    )


def project_kernel(terms, shards, sides, me_ref, *refs):
    acts, sources, out_refs = refs[:terms], refs[terms : 2 * terms], refs[2 * terms :]
    part = sources[0].shape[1] // shards
    for side, out_ref in zip(sides, out_refs):
        for i in range(shards // 2):
            start = pl.multiple_of(jnp.bitwise_xor(me_ref[0], 2 * i + side) * part, part)
            cut = pl.ds(start, part)
            total = contract(acts[0][...], sources[0][:, cut], 1, 0)
            for t in range(1, terms):
                total = total + contract(acts[t][...], sources[t][:, cut], 1, 0)
            out_ref[:, i * part : (i + 1) * part] = total.astype(BF16)


def project(me, acts, matrices, shards, sides):
    rows, model = acts[0].shape[0], matrices[0].shape[1]
    kernel = functools.partial(project_kernel, len(acts), shards, sides)
    return call(kernel, [(rows, model // 2)] * len(sides), me, [*acts, *matrices])


def turn_kernel(count, me_ref, *refs):
    hidden_ref, frames_out, hidden_out = refs[count:]
    part = refs[0].shape[1]
    for j in range(count):
        start = pl.multiple_of(jnp.bitwise_xor(me_ref[0], j) * part, part)
        frames_out[pl.ds(start, part), :] = jnp.transpose(refs[j][...])
    hidden_out[...] = jnp.transpose(hidden_ref[...])


def turn(me, frames, hidden):
    (rows, inner), count = hidden.shape, len(frames)
    shapes = [(count * frames[0].shape[1], rows), (inner, rows)]
    return call(functools.partial(turn_kernel, count), shapes, me, [*frames, hidden])


COPIES = 4


def weight_kernel(groups, rows, products, me_ref, *refs):
    lefts, refs = refs[:groups], refs[groups:]
    rights, refs = refs[: groups * sum(products)], refs[groups * sum(products) :]
    outs, staged, sems = refs[:-2], refs[-2], refs[-1]
    copies = []
    for out, count in zip(outs, products):
        pieces, rights = rights[: groups * count], rights[groups * count :]
        for top in range(0, out.shape[0], rows):
            at = len(copies) // COPIES
            left = jnp.concatenate([ref[top : top + rows, :] for ref in lefts], axis=1)
            for j in range(count):
                right = stacked(pieces[j * groups : (j + 1) * groups], 0)
                width = out.shape[1] // count
                start = j * width
                if count > 1:
                    start = pl.multiple_of(jnp.bitwise_xor(me_ref[0], j) * width, width)
                for cut in range(0, width, 256):
                    staged[at, :, pl.ds(start + cut, 256)] = contract(
                        left, right[:, cut : cut + 256], 1, 0
                    ).astype(BF16)
            size = rows // COPIES
            for i in range(COPIES):
                copy = pltpu.make_async_copy(
                    staged.at[at, pl.ds(i * size, size), :],
                    out.at[pl.ds(top + i * size, size), :],
                    sems.at[at, i],
                )
                copy.start()
                copies.append(copy)
    for copy in copies:
        copy.wait()


def weight_grads(me, lefts, rights, shape, rows):
    blocks = len(rights) * shape[0] // rows
    operands = [*lefts, *(group for entry in rights for block in entry for group in block)]
    products = [len(entry) for entry in rights]
    return pl.pallas_call(
        functools.partial(weight_kernel, len(lefts), rows, products),
        out_shape=[jax.ShapeDtypeStruct(shape, BF16)] * len(rights),
        in_specs=[scalar_block()] + [whole_block()] * len(operands),
        out_specs=[pl.BlockSpec(memory_space=pltpu.HBM)] * len(rights),
        scratch_shapes=[
            pltpu.VMEM((blocks, rows, shape[1]), BF16),
            pltpu.SemaphoreType.DMA((blocks, COPIES)),
        ],
        compiler_params=pltpu.CompilerParams(vmem_limit_bytes=VMEM_LIMIT),
        cost_estimate=COST,
    )(me, *operands)


def swap(value, axis, bit):
    pairs = [(i, i ^ bit) for i in range(lax.axis_size(axis))]
    return lax.ppermute(value, axis, pairs)


def gathered(own, shards):
    parts, bit = {0: own}, shards // 2
    while bit:
        for j, value in list(parts.items()):
            parts[j ^ bit] = swap(value, "shard", bit)
        bit //= 2
    return [parts[j] for j in range(shards)]


def scattered(send, keep, shards):
    arrived = swap(send, "shard", 1)
    total = (keep.astype(F32) + arrived.astype(F32)).astype(BF16)
    width, bit = total.shape[1], 2
    while bit < shards:
        width //= 2
        sent = swap(total[:, width:], "shard", bit)
        total = (total[:, :width].astype(F32) + sent.astype(F32)).astype(BF16)
        bit *= 2
    return total


def fast_device(frames, expert_ids, gate_weights, cotangent, weight_gate, weight_up, weight_down):
    experts, shards = lax.axis_size("expert"), lax.axis_size("shard")
    tok_rows, part = frames.shape
    capacity = 3 * tok_rows // experts
    expert_at = lax.axis_index("expert").astype(I32).reshape(1)
    me = lax.axis_index("shard").astype(I32).reshape(1)
    ids, gates = expert_ids.T, gate_weights.T
    gate, up, down = weight_gate[0], weight_up[0], weight_down[0]
    tile = 256
    half = experts // 2

    sent = dispatch(expert_at, me, ids, gates, frames, cotangent, experts, capacity)
    got = {0: sent[0]}
    for k in range(1, experts):
        got[k] = swap(sent[k], "expert", k)
    near_frames, near_cot = split(me, [got[k] for k in range(half)], part)
    picks = select(expert_at, ids, experts, capacity)
    kept = prepare([gate, up, down])
    gate, up, down, gate_turned, up_turned, down_turned = kept
    far_frames, far_cot = split(me, [got[k] for k in range(half, experts)], part)
    near_frames, near_cot = gathered(near_frames, shards), gathered(near_cot, shards)
    far_frames, far_cot = gathered(far_frames, shards), gathered(far_cot, shards)

    hidden_n, slope_n, silu_n = forward(me, near_frames, part, gate, up, tile)
    hidden_f, slope_f, silu_f = forward(me, far_frames, part, gate, up, tile)
    out_f = project(me, [hidden_f], [down], shards, (1, 0))
    grads_f = backward(me, far_cot, part, down_turned, slope_f, silu_f, tile)
    turned = [gate_turned, up_turned]
    back_f = [
        *project(me, grads_f, turned, shards, (1,)), *project(me, grads_f, turned, shards, (0,))
    ]
    out_n = project(me, [hidden_n], [down], shards, (1, 0))
    grads_n = backward(me, near_cot, part, down_turned, slope_n, silu_n, tile)
    back_n = [
        *project(me, grads_n, turned, shards, (1,)), *project(me, grads_n, turned, shards, (0,))
    ]
    frames_n, turned_n = turn(me, near_frames, hidden_n)
    frames_f, turned_f = turn(me, far_frames, hidden_f)
    shape, rows = gate.shape, 512
    (grad_down,) = weight_grads(
        me, [turned_n, turned_f], [list(zip(near_cot, far_cot))], shape[::-1], rows
    )
    grad_gate, grad_up = weight_grads(
        me, [frames_n, frames_f], [[pair] for pair in zip(grads_n, grads_f)], shape, rows
    )

    returned = {}
    for far, (out, back) in ((1, (out_f, back_f)), (0, (out_n, back_n))):
        both = jnp.concatenate([scattered(*out, shards), scattered(*back, shards)], axis=1)
        for i in range(half):
            k = far * half + i
            piece = both[i * capacity : (i + 1) * capacity]
            returned[k] = swap(piece, "expert", k) if k else piece
    combined, frame_grad = combine(me, picks, gates, [returned[k] for k in range(experts)])
    return combined, frame_grad, grad_gate[None], grad_up[None], grad_down[None]


def route_slot(flat_ids, experts):
    table = (flat_ids[:, None] == jnp.arange(experts, dtype=jnp.int32)[None, :]).astype(jnp.int32)
    earlier = jnp.cumsum(table, axis=0) - table
    return jnp.sum(earlier * table, axis=1)


def plain_device(frames, expert_ids, gate_weights, cotangent, weight_gate, weight_up, weight_down):
    experts = lax.axis_size("expert")
    tok_rows = frames.shape[0]
    top_count = expert_ids.shape[1]
    capacity = 3 * tok_rows // experts
    total_rows = experts * capacity
    part = frames.shape[1]
    flat_ids = expert_ids.reshape(-1)
    targets = flat_ids * capacity + route_slot(flat_ids, experts)
    weights_flat = gate_weights.reshape(-1, 1)
    gate, up, down = weight_gate[0], weight_up[0], weight_down[0]

    def exchange(values):
        return lax.all_to_all(values, "expert", split_axis=0, concat_axis=0, tiled=True)

    def place_rows(values):
        return jnp.zeros((total_rows, part), values.dtype).at[targets].set(values)

    frame_rows = jnp.repeat(frames, top_count, axis=0)
    cot_rows = jnp.repeat(cotangent, top_count, axis=0).astype(F32) * weights_flat
    inputs, routed = (
        lax.all_gather(exchange(place_rows(rows)), "shard", axis=1, tiled=True)
        for rows in (frame_rows, cot_rows.astype(BF16))
    )
    gate_act, up_act = contract(inputs, gate, 1, 0), contract(inputs, up, 1, 0)
    sigma = jax.nn.sigmoid(gate_act)
    hidden = (gate_act * sigma * up_act).astype(BF16)
    out_part = contract(hidden, down, 1, 0)
    hidden_grad = contract(routed, down, 1, 1)
    grad_down = contract(hidden, routed, 0, 0).astype(BF16)
    gate_grad = (hidden_grad * up_act * sigma * (1.0 + gate_act * (1.0 - sigma))).astype(BF16)
    up_grad = (hidden_grad * gate_act * sigma).astype(BF16)
    grad_gate = contract(inputs, gate_grad, 0, 0).astype(BF16)
    grad_up = contract(inputs, up_grad, 0, 0).astype(BF16)
    back_part = contract(gate_grad, gate, 1, 1) + contract(up_grad, up, 1, 1)
    picked_out, picked_back = (
        exchange(
            lax.psum_scatter(rows.astype(BF16), "shard", scatter_dimension=1, tiled=True)
        )[targets].astype(F32)
        for rows in (out_part, back_part)
    )
    combined = jnp.sum((picked_out * weights_flat).reshape(tok_rows, top_count, part), axis=1)
    frame_grad = jnp.sum(picked_back.reshape(tok_rows, top_count, part), axis=1)
    return (
        combined.astype(BF16),
        frame_grad.astype(BF16),
        grad_gate[None],
        grad_up[None],
        grad_down[None],
    )


def per_device(frames, *rest):
    experts, shards = lax.axis_size("expert"), lax.axis_size("shard")
    capacity = 3 * frames.shape[0] // experts
    fits = (
        frames.shape[1] % 128 == 0
        and frames.shape[0] % 128 == 0
        and capacity % 8 == 0
        and experts & (experts - 1) == 0
        and shards & (shards - 1) == 0
    )
    return (fast_device if fits else plain_device)(frames, *rest)


def solution(mesh):
    in_specs = (
        P("expert", "shard"),
        P("expert", None),
        P("expert", None),
        P("expert", "shard"),
        P("expert", None, "shard"),
        P("expert", None, "shard"),
        P("expert", "shard", None),
    )
    out_specs = (
        P("expert", "shard"),
        P("expert", "shard"),
        P("expert", None, "shard"),
        P("expert", None, "shard"),
        P("expert", "shard", None),
    )
    return jax.shard_map(
        per_device, mesh=mesh, in_specs=in_specs, out_specs=out_specs, check_vma=False
    )
```

```python
import functools

import jax
import jax.numpy as jnp
from jax import lax
from jax.experimental import pallas as pl
from jax.experimental.pallas import tpu as pltpu
from jax.sharding import PartitionSpec as P


F32, BF16, I32 = jnp.float32, jnp.bfloat16, jnp.int32
VMEM_LIMIT = 12 * 1024 * 1024


def contract(left, right, left_dim, right_dim):
    return lax.dot_general(
        left, right, (((left_dim,), (right_dim,)), ((), ())), preferred_element_type=F32
    )


def whole_block():
    return pl.BlockSpec(memory_space=pltpu.VMEM)


def scalar_block():
    return pl.BlockSpec(memory_space=pltpu.SMEM)


def selection(me, ids, experts, capacity):
    tok = ids.shape[1]
    expert_of = jnp.bitwise_xor(lax.broadcasted_iota(I32, (experts, tok), 0), me)
    first = ids[0:1, :] == expert_of
    second = ids[1:2, :] == expert_of
    table = jnp.where(first | second, 1.0, 0.0)
    upper = jnp.where(
        lax.broadcasted_iota(I32, (tok, tok), 0) < lax.broadcasted_iota(I32, (tok, tok), 1),
        1.0,
        0.0,
    )
    earlier = contract(table.astype(BF16), upper.astype(BF16), 1, 0).astype(I32)
    slot_first = jnp.where(first, earlier, -1)
    slot_second = jnp.where(second, earlier, -1)

    def one_hot(slots, k):
        rows = lax.broadcasted_iota(I32, (capacity, tok), 0)
        return jnp.where(slots[k : k + 1, :] == rows, 1.0, 0.0).astype(BF16)

    return slot_first, slot_second, one_hot


def dispatch_kernel(me_ref, _, *refs):
    sources, refs = refs[:4], refs[4:]
    send_refs, locals_, sems = refs[:-5], refs[-5:-1], refs[-1]
    copies = [
        pltpu.make_async_copy(source, local, sems.at[i])
        for i, (source, local) in enumerate(zip(sources, locals_))
    ]
    for copy in copies:
        copy.start()
    experts, capacity = len(send_refs), send_refs[0].shape[0]
    ids_ref, gates_ref, frames_ref, cot_ref = locals_
    width = frames_ref.shape[1]
    copies[0].wait()
    slot_first, slot_second, one_hot = selection(me_ref[0], ids_ref[...], experts, capacity)
    for copy in copies[1:]:
        copy.wait()
    gates = jnp.transpose(jnp.concatenate([gates_ref[...]] * 4, axis=0))
    cot = cot_ref[...].astype(F32)
    weighted = jnp.concatenate(
        [(cot * gates[:, 0:1]).astype(BF16), (cot * gates[:, 1:2]).astype(BF16)], axis=0
    )
    frames = frames_ref[...]
    for k in range(experts):
        first, second = one_hot(slot_first, k), one_hot(slot_second, k)
        send_refs[k][:, :width] = contract(first + second, frames, 1, 0).astype(BF16)
        send_refs[k][:, width:] = contract(
            jnp.concatenate([first, second], axis=1), weighted, 1, 0
        ).astype(BF16)


def dispatch(me, place, ids, gates, frames, cot, experts, capacity):
    width = 2 * frames.shape[1]
    sources = (ids, gates, frames, cot)
    return pl.pallas_call(
        dispatch_kernel,
        out_shape=[jax.ShapeDtypeStruct((capacity, width), BF16)] * experts,
        in_specs=[scalar_block()] * 2 + [pl.BlockSpec(memory_space=pltpu.HBM)] * 4,
        out_specs=[whole_block()] * experts,
        scratch_shapes=[pltpu.VMEM(a.shape, a.dtype) for a in sources]
        + [pltpu.SemaphoreType.DMA((4,))],
        compiler_params=pltpu.CompilerParams(vmem_limit_bytes=VMEM_LIMIT),
        name="dispatch",
    )(me, place, *(held(a) for a in sources))


def select_kernel(experts, me_ref, ids_ref, *turned_refs):
    capacity = turned_refs[0].shape[1] // experts
    *slots, one_hot = selection(me_ref[0], ids_ref[...], experts, capacity)
    for slot, turned_ref in zip(slots, turned_refs):
        rows = jnp.concatenate([one_hot(slot, k) for k in range(experts)], axis=0)
        turned_ref[...] = jnp.transpose(rows)


def select(me, ids, experts, capacity):
    kernel = functools.partial(select_kernel, experts)
    return call(kernel, [(ids.shape[1], experts * capacity)] * 2, me, [ids])


def combine_kernel(_, first_ref, second_ref, gates_ref, *refs):
    got_refs, (combined_ref, grad_ref) = refs[:-2], refs[-2:]
    width = combined_ref.shape[1]
    gates = jnp.transpose(jnp.concatenate([gates_ref[...]] * 4, axis=0))
    got = stacked(got_refs, 0)
    first = contract(first_ref[...], got, 1, 0)
    second = contract(second_ref[...], got, 1, 0)
    combined_ref[...] = (
        first[:, :width] * gates[:, 0:1] + second[:, :width] * gates[:, 1:2]
    ).astype(BF16)
    grad_ref[...] = (first[:, width:] + second[:, width:]).astype(BF16)


def combine(me, picks, gates, got):
    shape = (gates.shape[1], got[0].shape[1] // 2)
    return call(combine_kernel, [shape] * 2, me, [*picks, gates, *got])


def stacked(refs, axis):
    return jnp.concatenate([ref[...] for ref in refs], axis=axis)


COST = pl.CostEstimate(flops=1 << 20, bytes_accessed=1 << 16, transcendentals=0)


def held(matrix):
    return pltpu.with_memory_space_constraint(matrix, pltpu.HBM)


def call(kernel, shapes, me, arrays, scratch=()):
    return pl.pallas_call(
        kernel,
        out_shape=[jax.ShapeDtypeStruct(shape, BF16) for shape in shapes],
        in_specs=[scalar_block()] + [whole_block()] * len(arrays),
        out_specs=[whole_block()] * len(shapes),
        scratch_shapes=scratch,
        compiler_params=pltpu.CompilerParams(vmem_limit_bytes=VMEM_LIMIT),
        cost_estimate=COST,
    )(me, *arrays)


def prepare_kernel(count, *refs):
    sources, kept, turned, sems = refs[:count], refs[count : 2 * count], refs[2 * count : -1], refs[-1]
    copies = [
        pltpu.make_async_copy(source, target, sems.at[i])
        for i, (source, target) in enumerate(zip(sources, kept))
    ]
    for copy in copies:
        copy.start()
    for copy, source, target in zip(copies, kept, turned):
        copy.wait()

        @pl.loop(0, source.shape[0] // 256)
        def _(i):
            start = pl.multiple_of(i * 256, 256)
            target[:, pl.ds(start, 256)] = jnp.transpose(source[pl.ds(start, 256), :])


def prepare(matrices):
    count = len(matrices)
    shapes = [m.shape for m in matrices] + [m.shape[::-1] for m in matrices]
    return pl.pallas_call(
        functools.partial(prepare_kernel, count),
        out_shape=[jax.ShapeDtypeStruct(shape, BF16) for shape in shapes],
        in_specs=[pl.BlockSpec(memory_space=pltpu.HBM)] * count,
        out_specs=[whole_block()] * (2 * count),
        scratch_shapes=[pltpu.SemaphoreType.DMA((count,))],
        compiler_params=pltpu.CompilerParams(vmem_limit_bytes=VMEM_LIMIT),
        cost_estimate=COST,
    )(*(held(m) for m in matrices))


def ordered(ref, me, count, cut):
    size = ref.shape[0] // count
    starts = [pl.multiple_of(jnp.bitwise_xor(me, j) * size, size) for j in range(count)]
    return jnp.concatenate([ref[pl.ds(start, size), cut] for start in starts], axis=0)


def split_kernel(part, me_ref, *refs):
    whole = stacked(refs[:-2], 0)
    refs[-2][...] = whole[:, :part]
    refs[-1][...] = whole[:, part:]


def split(me, pieces, part):
    rows = sum(p.shape[0] for p in pieces)
    kernel = functools.partial(split_kernel, part)
    return call(kernel, [(rows, part)] * 2, me, pieces)


def forward_kernel(count, part, tile, me_ref, *refs):
    gate_ref, up_ref, hidden_ref, slope_ref, silu_ref, gate_sum, up_sum = refs[count:]
    me = me_ref[0]
    tiles = hidden_ref.shape[1] // tile
    inputs = jnp.concatenate([ref[:, :part] for ref in refs[:count]], axis=1)

    def finish(i):
        cut = slice(i * tile, (i + 1) * tile)
        gate_act, up_act = gate_sum[i % 2], up_sum[i % 2]
        sigma = jax.nn.sigmoid(gate_act)
        silu = gate_act * sigma
        hidden_ref[:, cut] = (silu * up_act).astype(BF16)
        silu_ref[:, cut] = silu.astype(BF16)
        slope_ref[:, cut] = (up_act * sigma * (1.0 + gate_act * (1.0 - sigma))).astype(BF16)

    for i in range(tiles):
        cut = slice(i * tile, (i + 1) * tile)
        gate_sum[i % 2] = contract(inputs, ordered(gate_ref, me, count, cut), 1, 0)
        up_sum[i % 2] = contract(inputs, ordered(up_ref, me, count, cut), 1, 0)
        if i:
            finish(i - 1)
    finish(tiles - 1)


def forward(me, parts, part, gate, up, tile):
    rows, (model, inner) = parts[0].shape[0], gate.shape
    return call(
        functools.partial(forward_kernel, len(parts), part, tile),
        [(rows, inner)] * 3,
        me,
        [*parts, gate, up],
        [pltpu.VMEM((2, rows, tile), F32)] * 2,
    )


def backward_kernel(count, part, tile, me_ref, *refs):
    slope_ref, silu_ref, turned_ref, gate_grad_ref, up_grad_ref, hidden_sum = refs[count:]
    me = me_ref[0]
    tiles = slope_ref.shape[1] // tile
    routed = jnp.concatenate([ref[:, ref.shape[1] - part :] for ref in refs[:count]], axis=1)

    def finish(i):
        cut = slice(i * tile, (i + 1) * tile)
        hidden_grad = hidden_sum[i % 2]
        gate_grad_ref[:, cut] = (hidden_grad * slope_ref[:, cut].astype(F32)).astype(BF16)
        up_grad_ref[:, cut] = (hidden_grad * silu_ref[:, cut].astype(F32)).astype(BF16)

    for i in range(tiles):
        cut = slice(i * tile, (i + 1) * tile)
        hidden_sum[i % 2] = contract(routed, ordered(turned_ref, me, count, cut), 1, 0)
        if i:
            finish(i - 1)
    finish(tiles - 1)


def backward(me, parts, part, down_turned, slope, silu, tile):
    rows, (model, inner) = parts[0].shape[0], down_turned.shape
    return call(
        functools.partial(backward_kernel, len(parts), part, tile),
        [(rows, inner)] * 2,
        me,
        [*parts, slope, silu, down_turned],
        [pltpu.VMEM((2, rows, tile), F32)],
    )


def project_kernel(terms, shards, sides, me_ref, *refs):
    acts, sources, out_refs = refs[:terms], refs[terms : 2 * terms], refs[2 * terms :]
    part = sources[0].shape[1] // shards
    for side, out_ref in zip(sides, out_refs):
        for i in range(shards // 2):
            start = pl.multiple_of(jnp.bitwise_xor(me_ref[0], 2 * i + side) * part, part)
            cut = pl.ds(start, part)
            total = contract(acts[0][...], sources[0][:, cut], 1, 0)
            for t in range(1, terms):
                total = total + contract(acts[t][...], sources[t][:, cut], 1, 0)
            out_ref[:, i * part : (i + 1) * part] = total.astype(BF16)


def project(me, acts, matrices, shards, sides):
    rows, model = acts[0].shape[0], matrices[0].shape[1]
    kernel = functools.partial(project_kernel, len(acts), shards, sides)
    return call(kernel, [(rows, model // 2)] * len(sides), me, [*acts, *matrices])


def turn_kernel(count, me_ref, *refs):
    hidden_ref, frames_out, hidden_out = refs[count:]
    part = refs[0].shape[1]
    for j in range(count):
        start = pl.multiple_of(jnp.bitwise_xor(me_ref[0], j) * part, part)
        frames_out[pl.ds(start, part), :] = jnp.transpose(refs[j][...])
    hidden_out[...] = jnp.transpose(hidden_ref[...])


def turn(me, frames, hidden):
    (rows, inner), count = hidden.shape, len(frames)
    shapes = [(count * frames[0].shape[1], rows), (inner, rows)]
    return call(functools.partial(turn_kernel, count), shapes, me, [*frames, hidden])


COPIES = 4


def weight_down_kernel(groups, rows, count, me_ref, *refs):
    lefts, rights, out = refs[:groups], refs[groups:-1], refs[-1]
    width = out.shape[1] // count
    for top in range(0, out.shape[0], rows):
        left = jnp.concatenate([ref[top : top + rows, :] for ref in lefts], axis=1)
        for j in range(count):
            start = pl.multiple_of(jnp.bitwise_xor(me_ref[0], j) * width, width)
            right = stacked(rights[j * groups : (j + 1) * groups], 0)
            out[top : top + rows, pl.ds(start, width)] = contract(left, right, 1, 0).astype(BF16)


def down_grads(me, lefts, rights, shape, rows):
    kernel = functools.partial(weight_down_kernel, len(lefts), rows, len(rights))
    operands = [*lefts, *(group for block in rights for group in block)]
    return call(kernel, [shape], me, operands)[0]


def weight_kernel(groups, rows, products, me_ref, ready_ref, *refs):
    ready_out, ready_sem = refs[-4], refs[-1]
    refs = (*refs[:-4], *refs[-3:-1])
    ready = pltpu.make_async_copy(ready_ref, ready_out, ready_sem)
    ready.start()
    lefts, refs = refs[:groups], refs[groups:]
    rights, refs = refs[: groups * sum(products)], refs[groups * sum(products) :]
    outs, staged, sems = refs[:-2], refs[-2], refs[-1]
    copies = []
    for out, count in zip(outs, products):
        pieces, rights = rights[: groups * count], rights[groups * count :]
        for top in range(0, out.shape[0], rows):
            at = len(copies) // COPIES
            left = jnp.concatenate([ref[top : top + rows, :] for ref in lefts], axis=1)
            for j in range(count):
                right = stacked(pieces[j * groups : (j + 1) * groups], 0)
                width = out.shape[1] // count
                start = j * width
                if count > 1:
                    start = pl.multiple_of(jnp.bitwise_xor(me_ref[0], j) * width, width)
                for cut in range(0, width, 256):
                    staged[at, :, pl.ds(start + cut, 256)] = contract(
                        left, right[:, cut : cut + 256], 1, 0
                    ).astype(BF16)
            size = rows // COPIES
            for i in range(COPIES):
                copy = pltpu.make_async_copy(
                    staged.at[at, pl.ds(i * size, size), :],
                    out.at[pl.ds(top + i * size, size), :],
                    sems.at[at, i],
                )
                copy.start()
                copies.append(copy)
    for copy in (*copies, ready):
        copy.wait()


def weight_grads(me, ready, lefts, rights, shape, rows):
    blocks = len(rights) * shape[0] // rows
    operands = [*lefts, *(group for entry in rights for block in entry for group in block)]
    products = [len(entry) for entry in rights]
    return pl.pallas_call(
        functools.partial(weight_kernel, len(lefts), rows, products),
        out_shape=[jax.ShapeDtypeStruct(shape, BF16)] * len(rights)
        + [jax.ShapeDtypeStruct(ready.shape, BF16)],
        in_specs=[scalar_block()] + [whole_block()] * (len(operands) + 1),
        out_specs=[pl.BlockSpec(memory_space=pltpu.HBM)] * (len(rights) + 1),
        scratch_shapes=[
            pltpu.VMEM((blocks, rows, shape[1]), BF16),
            pltpu.SemaphoreType.DMA((blocks, COPIES)),
            pltpu.SemaphoreType.DMA,
        ],
        compiler_params=pltpu.CompilerParams(vmem_limit_bytes=VMEM_LIMIT),
        cost_estimate=COST,
    )(me, ready, *operands)


def swap(value, axis, bit):
    pairs = [(i, i ^ bit) for i in range(lax.axis_size(axis))]
    return lax.ppermute(value, axis, pairs)


def gathered(own, shards):
    parts, bit = {0: own}, shards // 2
    while bit:
        for j, value in list(parts.items()):
            parts[j ^ bit] = swap(value, "shard", bit)
        bit //= 2
    return [parts[j] for j in range(shards)]


def scattered(send, keep, shards):
    arrived = swap(send, "shard", 1)
    total = (keep.astype(F32) + arrived.astype(F32)).astype(BF16)
    width, bit = total.shape[1], 2
    while bit < shards:
        width //= 2
        sent = swap(total[:, width:], "shard", bit)
        total = (total[:, :width].astype(F32) + sent.astype(F32)).astype(BF16)
        bit *= 2
    return total


def fast_device(frames, expert_ids, gate_weights, cotangent, weight_gate, weight_up, weight_down):
    experts, shards = lax.axis_size("expert"), lax.axis_size("shard")
    tok_rows, part = frames.shape
    capacity = 3 * tok_rows // experts
    expert_at = lax.axis_index("expert").astype(I32).reshape(1)
    me = lax.axis_index("shard").astype(I32).reshape(1)
    ids, gates = expert_ids.T, gate_weights.T
    gate, up, down = weight_gate[0], weight_up[0], weight_down[0]
    tile = 256
    half = experts // 2

    sent = dispatch(expert_at, me, ids, gates, frames, cotangent, experts, capacity)
    got = {0: sent[0]}
    for k in range(1, experts):
        got[k] = swap(sent[k], "expert", k)
    near_frames, near_cot = split(me, [got[k] for k in range(half)], part)
    picks = select(expert_at, ids, experts, capacity)
    kept = prepare([gate, up, down])
    gate, up, down, gate_turned, up_turned, down_turned = kept
    far_frames, far_cot = split(me, [got[k] for k in range(half, experts)], part)
    near_frames, near_cot = gathered(near_frames, shards), gathered(near_cot, shards)
    far_frames, far_cot = gathered(far_frames, shards), gathered(far_cot, shards)

    hidden_n, slope_n, silu_n = forward(me, near_frames, part, gate, up, tile)
    hidden_f, slope_f, silu_f = forward(me, far_frames, part, gate, up, tile)
    out_f = project(me, [hidden_f], [down], shards, (1, 0))
    grads_f = backward(me, far_cot, part, down_turned, slope_f, silu_f, tile)
    turned = [gate_turned, up_turned]
    back_f = [
        *project(me, grads_f, turned, shards, (1,)), *project(me, grads_f, turned, shards, (0,))
    ]
    out_n = project(me, [hidden_n], [down], shards, (1, 0))
    grads_n = backward(me, near_cot, part, down_turned, slope_n, silu_n, tile)
    back_n = [
        *project(me, grads_n, turned, shards, (1,)), *project(me, grads_n, turned, shards, (0,))
    ]
    frames_n, turned_n = turn(me, near_frames, hidden_n)
    frames_f, turned_f = turn(me, far_frames, hidden_f)
    shape, rows = gate.shape, 512
    down_ready = down_grads(
        me, [turned_n, turned_f], list(zip(near_cot, far_cot)), shape[::-1], rows
    )
    grad_gate, grad_up, grad_down = weight_grads(
        me,
        down_ready,
        [frames_n, frames_f],
        [[pair] for pair in zip(grads_n, grads_f)],
        shape,
        rows,
    )

    returned = {}
    for far, (out, back) in ((1, (out_f, back_f)), (0, (out_n, back_n))):
        both = jnp.concatenate([scattered(*out, shards), scattered(*back, shards)], axis=1)
        for i in range(half):
            k = far * half + i
            piece = both[i * capacity : (i + 1) * capacity]
            returned[k] = swap(piece, "expert", k) if k else piece
    combined, frame_grad = combine(me, picks, gates, [returned[k] for k in range(experts)])
    return combined, frame_grad, grad_gate[None], grad_up[None], grad_down[None]


def route_slot(flat_ids, experts):
    table = (flat_ids[:, None] == jnp.arange(experts, dtype=jnp.int32)[None, :]).astype(jnp.int32)
    earlier = jnp.cumsum(table, axis=0) - table
    return jnp.sum(earlier * table, axis=1)


def plain_device(frames, expert_ids, gate_weights, cotangent, weight_gate, weight_up, weight_down):
    experts = lax.axis_size("expert")
    tok_rows = frames.shape[0]
    top_count = expert_ids.shape[1]
    capacity = 3 * tok_rows // experts
    total_rows = experts * capacity
    part = frames.shape[1]
    flat_ids = expert_ids.reshape(-1)
    targets = flat_ids * capacity + route_slot(flat_ids, experts)
    weights_flat = gate_weights.reshape(-1, 1)
    gate, up, down = weight_gate[0], weight_up[0], weight_down[0]

    def exchange(values):
        return lax.all_to_all(values, "expert", split_axis=0, concat_axis=0, tiled=True)

    def place_rows(values):
        return jnp.zeros((total_rows, part), values.dtype).at[targets].set(values)

    frame_rows = jnp.repeat(frames, top_count, axis=0)
    cot_rows = jnp.repeat(cotangent, top_count, axis=0).astype(F32) * weights_flat
    inputs, routed = (
        lax.all_gather(exchange(place_rows(rows)), "shard", axis=1, tiled=True)
        for rows in (frame_rows, cot_rows.astype(BF16))
    )
    gate_act, up_act = contract(inputs, gate, 1, 0), contract(inputs, up, 1, 0)
    sigma = jax.nn.sigmoid(gate_act)
    hidden = (gate_act * sigma * up_act).astype(BF16)
    out_part = contract(hidden, down, 1, 0)
    hidden_grad = contract(routed, down, 1, 1)
    grad_down = contract(hidden, routed, 0, 0).astype(BF16)
    gate_grad = (hidden_grad * up_act * sigma * (1.0 + gate_act * (1.0 - sigma))).astype(BF16)
    up_grad = (hidden_grad * gate_act * sigma).astype(BF16)
    grad_gate = contract(inputs, gate_grad, 0, 0).astype(BF16)
    grad_up = contract(inputs, up_grad, 0, 0).astype(BF16)
    back_part = contract(gate_grad, gate, 1, 1) + contract(up_grad, up, 1, 1)
    picked_out, picked_back = (
        exchange(
            lax.psum_scatter(rows.astype(BF16), "shard", scatter_dimension=1, tiled=True)
        )[targets].astype(F32)
        for rows in (out_part, back_part)
    )
    combined = jnp.sum((picked_out * weights_flat).reshape(tok_rows, top_count, part), axis=1)
    frame_grad = jnp.sum(picked_back.reshape(tok_rows, top_count, part), axis=1)
    return (
        combined.astype(BF16),
        frame_grad.astype(BF16),
        grad_gate[None],
        grad_up[None],
        grad_down[None],
    )


def per_device(frames, *rest):
    experts, shards = lax.axis_size("expert"), lax.axis_size("shard")
    capacity = 3 * frames.shape[0] // experts
    fits = (
        frames.shape[1] % 128 == 0
        and frames.shape[0] % 128 == 0
        and capacity % 8 == 0
        and experts & (experts - 1) == 0
        and shards & (shards - 1) == 0
    )
    return (fast_device if fits else plain_device)(frames, *rest)


def solution(mesh):
    in_specs = (
        P("expert", "shard"),
        P("expert", None),
        P("expert", None),
        P("expert", "shard"),
        P("expert", None, "shard"),
        P("expert", None, "shard"),
        P("expert", "shard", None),
    )
    out_specs = (
        P("expert", "shard"),
        P("expert", "shard"),
        P("expert", None, "shard"),
        P("expert", None, "shard"),
        P("expert", "shard", None),
    )
    return jax.shard_map(
        per_device, mesh=mesh, in_specs=in_specs, out_specs=out_specs, check_vma=False
    )
```
